128 devices in a mesh: section: 4 (over x), dp: 8 (over z_lo, y), tensor: 4 (over z_hi, core).
Axes of the slice: x: 4, y: 4, z: 4 (z_hi: 2, z_lo: 2; z = z_hi * 2 + z_lo), core: 2. Of those that a mesh axis runs over, the one named last changes fastest.
Arguments:
- saved: bfloat16 [4, 4096, 5120], P('section', ('dp', 'tensor')), may hold values from -0.09375 to 0.09375
- weight: bfloat16 [4, 5120, 5120], P('section', None, 'tensor'), may hold values from -0.078125 to 0.078125
- out_grad: bfloat16 [4096, 5120], P(('dp', 'tensor')), may hold values from -6 to 6
Outputs:
- input_grads: bfloat16 [4, 4096, 5120], P('section', ('dp', 'tensor'))
- weight_grads: float32 [4, 5120, 5120], P('section', 'dp', 'tensor')
The draws below stay inside these ranges and needn't reach their ends.
All inputs are finite; a program needn't handle non-finite values.
Results may differ from the reference program's by a relative error of at most 0.02.
Values may be sent and summed in bfloat16 or wider, within the bound.
A program may use at most 192 MiB of HBM per device.

```python
import jax
import jax.numpy as jnp
from jax import lax

D = 5120
SEQ = 512
TOKENS = 4096
N_SECTION = 4
N_DP = 8
N_TENSOR = 4


def levels(key, dims, split, least, largest):
    level, own = 1.0, jax.random.fold_in(key, 6)
    for axis_at, parts in split:
        steps = jnp.exp(jax.random.uniform(jax.random.fold_in(own, axis_at), (parts,), jnp.float32, least / len(split), largest / len(split)))
        level = level * jnp.repeat(steps, dims[axis_at] // parts).reshape([-1 if axis == axis_at else 1 for axis in range(len(dims))])
    return level


def gaussian(key, dims, scale, reach, split=(), kind=jnp.bfloat16):
    values = scale * jax.random.normal(key, dims, jnp.float32)
    if split:
        values = values * levels(key, dims, split, -0.22, 0.18)
    return jnp.clip(values, -reach, reach).astype(kind)


def setup_inputs(seed: int = 0) -> dict:
    arg_keys = jax.random.split(jax.random.key(seed), 4)
    saved = gaussian(arg_keys[0], (N_SECTION, TOKENS, D), (TOKENS ** -0.5), 0.09375, ((0, 4), (1, 32)))
    weight = gaussian(arg_keys[1], (N_SECTION, D, D), D ** -0.5, 0.078125, ((0, 4), (2, 4)))
    out_grad = gaussian(arg_keys[2], (TOKENS, D), 1.0, 6.0, ((0, 32),))
    return dict(saved=saved, weight=weight, out_grad=out_grad)


def reference(saved, weight, out_grad):
    width = D // N_TENSOR
    gradient = out_grad
    input_list = [None] * N_SECTION
    weight_list = [None] * N_SECTION
    for layer_section in reversed(range(N_SECTION)):
        matrix = weight[layer_section]
        total = jnp.zeros((TOKENS, D), jnp.float32)
        for column_block in range(N_TENSOR):
            grad_block = gradient[:, column_block * width:(column_block + 1) * width]
            weight_block = matrix[:, column_block * width:(column_block + 1) * width]
            partial_sum = jnp.dot(grad_block, weight_block.T, preferred_element_type=jnp.float32)
            partial_sum = lax.optimization_barrier(partial_sum.astype(jnp.bfloat16)).astype(jnp.float32)
            total = total + partial_sum
        updated = (gradient.astype(jnp.float32) + total).astype(jnp.bfloat16)
        summed = jnp.zeros((D, D), jnp.float32)
        for replica in range(N_DP):
            inputs_q = saved[layer_section, replica * SEQ:(replica + 1) * SEQ]
            grads_q = gradient[replica * SEQ:(replica + 1) * SEQ]
            seq_part = jnp.dot(inputs_q.T, grads_q, preferred_element_type=jnp.float32)
            seq_part = lax.optimization_barrier(seq_part.astype(jnp.bfloat16)).astype(jnp.float32)
            summed = summed + seq_part
        input_list[layer_section] = updated
        weight_list[layer_section] = summed
        gradient = updated
    return jnp.stack(input_list), jnp.stack(weight_list)
```

```python
import functools

import jax
import jax.numpy as jnp
from jax import lax
from jax.experimental import pallas as pl
from jax.experimental.pallas import tpu as pltpu
from jax.sharding import PartitionSpec as P

MESH = pl.DeviceIdType.MESH
BF16 = jnp.bfloat16
F32 = jnp.float32
CW = 256
NY = 4


def rdma(src, dst, send, recv, dev):
    return pltpu.make_async_remote_copy(
        src_ref=src, dst_ref=dst, send_sem=send, recv_sem=recv, device_id=dev, device_id_type=MESH
    )


def nt_dot(a, b):
    return lax.dot_general(a, b, (((1,), (1,)), ((), ())), preferred_element_type=F32)


def relay(
    og, w,
    out, gq,
    wv, g, ps, pr, own, gn,
    w_sem, w_send, w_recv, gi_send, gi_recv, x_recv, f_send, f_recv, p_send, p_recv, x_send, o_send, o_recv, loc,
):
    rows, width = og.shape
    quarter = width // 4
    half = width // 2
    nk = quarter // CW
    sections = lax.axis_size("section")
    s, d, t = lax.axis_index("section"), lax.axis_index("dp"), lax.axis_index("tensor")
    l, y = d // NY, d % NY
    h, c = t // 2, t % 2
    partner = (s, d, h * 2 + 1 - c)
    pair_t = (1 - h) * 2 + c
    pair_d = (1 - l) * NY + y
    pair = (s, pair_d, pair_t)
    pair_x = (s, pair_d, (1 - h) * 2 + 1 - c)
    up = (lax.rem(s + sections - 1, sections), d, t)
    down = (lax.rem(s + 1, sections), d, t)
    first = s == sections - 1

    barrier = pltpu.get_barrier_semaphore()
    for dev in (partner, pair, pair_x, up, down):
        pl.semaphore_signal(barrier, inc=1, device_id=dev, device_id_type=MESH)
    pl.semaphore_wait(barrier, 5)

    cols = pl.ds(pl.multiple_of(c * quarter, quarter), quarter)

    def w_rows(a, core):
        hh = (1 - h) if a == 0 else h
        return pl.ds(pl.multiple_of(hh * half + core * quarter, quarter), quarter)

    w_local = [pltpu.make_async_copy(w.at[w_rows(a, c), :], wv.at[a, :, cols], w_sem.at[a]) for a in range(2)]
    w_away = [rdma(w.at[w_rows(a, 1 - c), :], wv.at[a, :, cols], w_send.at[a], w_recv.at[a], partner) for a in range(2)]
    own_rows = pl.ds(pl.multiple_of(t * rows, rows), rows)
    pair_rows = pl.ds(pl.multiple_of(pair_t * rows, rows), rows)
    my_half = pl.ds(pl.multiple_of(h * half, half), half)
    other_half = pl.ds(pl.multiple_of((1 - h) * half, half), half)
    g_pair = rdma(og.at[:, other_half], g.at[own_rows, :], gi_send.at[0], gi_recv.at[0], pair)
    g_partner = rdma(og.at[:, my_half], g.at[own_rows, :], gi_send.at[1], gi_recv.at[1], partner)
    g_fwd = rdma(g.at[pair_rows, :], g.at[pair_rows, :], gi_send.at[2], gi_recv.at[2], partner)

    @pl.when(first)
    def _():
        g_pair.start()
        g_partner.start()

    for a in range(2):
        w_away[a].start()
        w_local[a].start()

    def x_cols(k):
        return pl.ds(pl.multiple_of(c * quarter + k * CW, CW), CW)

    def x_copy(k):
        return rdma(
            gn.at[:, pl.ds(pl.multiple_of(k * CW, CW), CW)], g.at[:, x_cols(k)], x_send.at[k], x_recv.at[k], up
        )

    def f_copy(k):
        return rdma(g.at[:, x_cols(k)], g.at[:, x_cols(k)], f_send.at[k], f_recv.at[k], partner)

    @pl.when(first)
    def _():
        here = pltpu.make_async_copy(og.at[:, my_half], g.at[own_rows, :], loc.at[0])
        here.start()
        g_pair.wait_recv()
        g_fwd.start()
        here.wait()
        g_partner.wait_recv()
        g_fwd.wait_recv()
        g_pair.wait_send()
        g_partner.wait_send()
        g_fwd.wait_send()

    @pl.when(jnp.logical_not(first))
    def _():
        def arrive(k, carry):
            x_copy(k).wait_recv()
            f_copy(k).start()
            return carry

        lax.fori_loop(0, nk, arrive, 0)

        def forwarded(k, carry):
            f_copy(k).wait_recv()
            f_copy(k).wait_send()
            return carry

        lax.fori_loop(0, nk, forwarded, 0)

    keep = pltpu.make_async_copy(g.at[:, cols], gq, loc.at[1])
    keep.start()

    for a in range(2):
        w_local[a].wait()
        w_away[a].wait_recv()
        w_away[a].wait_send()

    def p_copy(k):
        return rdma(ps.at[k], pr.at[k], p_send.at[k], p_recv.at[k], pair)

    def send_part(k, carry):
        ps[k] = nt_dot(g[...], wv[0, pl.ds(pl.multiple_of(k * CW, CW), CW), :]).astype(BF16)
        p_copy(k).start()
        return carry

    lax.fori_loop(0, nk, send_part, 0)

    def own_part(k, carry):
        own[k] = nt_dot(g[...], wv[1, pl.ds(pl.multiple_of(k * CW, CW), CW), :])
        return carry

    lax.fori_loop(0, nk, own_part, 0)

    def finish(k, carry):
        p_copy(k).wait_recv()
        total = own[k] + pr[k].astype(F32) + g[:, x_cols(k)].astype(F32)
        gn[:, pl.ds(pl.multiple_of(k * CW, CW), CW)] = total.astype(BF16)

        @pl.when(s > 0)
        def _():
            x_copy(k).start()

        return carry

    lax.fori_loop(0, nk, finish, 0)

    t_cols = pl.ds(pl.multiple_of(t * quarter, quarter), quarter)
    homes = [partner, pair, pair_x]
    blocks = [h * 2 + 1 - c, pair_t, (1 - h) * 2 + 1 - c]
    home = [
        rdma(gn.at[pl.ds(pl.multiple_of(b * rows, rows), rows), :], out.at[:, t_cols], o_send.at[i], o_recv.at[i], dev)
        for i, (dev, b) in enumerate(zip(homes, blocks))
    ]
    for copy in home:
        copy.start()
    mine = pltpu.make_async_copy(gn.at[own_rows, :], out.at[:, t_cols], loc.at[0])
    mine.start()
    mine.wait()
    keep.wait()
    for copy in home:
        copy.wait_recv()
        copy.wait_send()

    def drain(k, carry):
        p_copy(k).wait_send()

        @pl.when(s > 0)
        def _():
            x_copy(k).wait_send()

        return carry

    lax.fori_loop(0, nk, drain, 0)


def on_device(saved, weight, out_grad):
    rows, width = out_grad.shape
    quarter, half = width // 4, width // 2
    nk = quarter // CW
    dma = pltpu.SemaphoreType.DMA
    vmem = pltpu.VMEM
    own_input, columns = pl.pallas_call(
        relay,
        out_shape=(
            jax.ShapeDtypeStruct((rows, width), BF16),
            jax.ShapeDtypeStruct((4 * rows, quarter), BF16),
        ),
        in_specs=[pl.BlockSpec(memory_space=pltpu.VMEM), pl.BlockSpec(memory_space=pl.ANY)],
        out_specs=(pl.BlockSpec(memory_space=pltpu.VMEM), pl.BlockSpec(memory_space=pltpu.VMEM)),
        scratch_shapes=[
            vmem((2, quarter, half), BF16),
            vmem((4 * rows, half), BF16),
            vmem((nk, 4 * rows, CW), BF16),
            vmem((nk, 4 * rows, CW), BF16),
            vmem((nk, 4 * rows, CW), F32),
            vmem((4 * rows, quarter), BF16),
            dma((2,)), dma((2,)), dma((2,)), dma((3,)), dma((3,)),
            dma((nk,)), dma((nk,)), dma((nk,)), dma((nk,)), dma((nk,)), dma((nk,)),
            dma((3,)), dma((3,)), dma((2,)),
        ],
        compiler_params=pltpu.CompilerParams(
            collective_id=0, has_side_effects=True, vmem_limit_bytes=60 * 1024 * 1024
        ),
    )(out_grad, weight[0])

    def pick(dp_flip, h_flip, c_flip):
        route = []
        for dd in range(8):
            for tt in range(4):
                ll, yy, hh, cc = dd // NY, dd % NY, tt // 2, tt % 2
                src = dd * 4 + tt
                dst = ((ll ^ dp_flip) * NY + yy) * 4 + (hh ^ h_flip) * 2 + (cc ^ c_flip)
                route.append((src, dst))
        return route

    mine = saved[0]
    others = [
        lax.ppermute(mine, ("dp", "tensor"), pick(*flips)) for flips in ((0, 0, 1), (1, 1, 0), (1, 1, 1))
    ]
    t = lax.axis_index("tensor")
    c = t % 2
    h = t // 2
    chip = jnp.where(c == 0, jnp.concatenate([mine, others[0]]), jnp.concatenate([others[0], mine]))
    pair = jnp.where(c == 0, jnp.concatenate([others[1], others[2]]), jnp.concatenate([others[2], others[1]]))
    gathered = jnp.where(h == 0, jnp.concatenate([chip, pair]), jnp.concatenate([pair, chip]))
    weight_grad = lax.psum_scatter(
        lax.dot_general(gathered, columns, (((0,), (0,)), ((), ())), preferred_element_type=F32).astype(BF16),
        "dp",
        scatter_dimension=0,
        tiled=True,
    ).astype(F32)
    return (own_input[None], weight_grad[None])


def solution(mesh):
    placed = (
        P("section", ("dp", "tensor"), None),
        P("section", None, "tensor"),
        P(("dp", "tensor"), None),
    )
    return jax.shard_map(
        on_device,
        mesh=mesh,
        in_specs=placed,
        out_specs=(P("section", ("dp", "tensor"), None), P("section", "dp", "tensor")),
        check_vma=False,
    )
```

```python
import jax
import jax.numpy as jnp
from jax import lax
from jax.experimental import pallas as pl
from jax.experimental.pallas import tpu as pltpu
from jax.sharding import PartitionSpec as P

MESH = pl.DeviceIdType.MESH
BF16 = jnp.bfloat16
F32 = jnp.float32
CW = 256
NY = 4
SKEW = 7


def rdma(src, dst, send, recv, dev):
    return pltpu.make_async_remote_copy(
        src_ref=src, dst_ref=dst, send_sem=send, recv_sem=recv, device_id=dev, device_id_type=MESH
    )


def nt_dot(a, b):
    return lax.dot_general(a, b, (((1,), (1,)), ((), ())), preferred_element_type=F32)


def tn_dot(a, b):
    return lax.dot_general(a, b, (((0,), (0,)), ((), ())), preferred_element_type=F32)


def span(start, size):
    return pl.ds(pl.multiple_of(start, 128), size)


def relay(
    og, w, saved,
    out, wg,
    wv, g, ps, pr, own, gn, gy, sv, lo, lr,
    w_sem, w_send, w_recv, gi_send, gi_recv, x_send, x_recv, f_send, f_recv, p_send, p_recv,
    o_send, o_recv, y_send, y_recv, r_send, r_recv, s_send, s_recv, t_send, t_recv, l_send, l_recv, loc, yloc,
):
    rows, width = og.shape
    quarter, half = width // 4, width // 2
    nk = quarter // CW
    pieces = 4
    total = pieces * nk
    block = quarter // 2
    sections = lax.axis_size("section")
    s, d, t = lax.axis_index("section"), lax.axis_index("dp"), lax.axis_index("tensor")
    l, y = d // NY, d % NY
    h, c = t // 2, t % 2
    partner_t = h * 2 + 1 - c
    pair_t = (1 - h) * 2 + c
    cross_t = (1 - h) * 2 + 1 - c
    pair_l = (1 - l) * NY
    partner = (s, d, partner_t)
    pair = (s, pair_l + y, pair_t)
    cross = (s, pair_l + y, cross_t)
    level = (s, pair_l + y, t)
    up = (lax.rem(s + sections - 1, sections), d, t)
    down = (lax.rem(s + 1, sections), d, t)
    first = s == sections - 1
    ys = [lax.rem(y + dy, NY) for dy in range(NY)]
    along = [(s, l * NY + ys[dy], t) for dy in range(NY)]
    pair_along = [(s, pair_l + ys[dy], pair_t) for dy in range(NY)]

    barrier = pltpu.get_barrier_semaphore()
    friends = [partner, pair, cross, level, up, down] + along[1:] + pair_along[1:]
    for dev in friends:
        pl.semaphore_signal(barrier, inc=1, device_id=dev, device_id_type=MESH)
    pl.semaphore_wait(barrier, len(friends))

    cols = span(c * quarter, quarter)
    t_cols = span(t * quarter, quarter)
    own_rows = span(t * rows, rows)
    pair_rows = span(pair_t * rows, rows)
    my_half = span(h * half, half)
    other_half = span((1 - h) * half, half)

    g_pair = rdma(og.at[:, other_half], g.at[own_rows, :], gi_send.at[0], gi_recv.at[0], pair)
    g_partner = rdma(og.at[:, my_half], g.at[own_rows, :], gi_send.at[1], gi_recv.at[1], partner)
    g_fwd = rdma(g.at[pair_rows, :], g.at[pair_rows, :], gi_send.at[2], gi_recv.at[2], partner)

    @pl.when(first)
    def _():
        g_pair.start()
        g_partner.start()

    def w_rows(a, core):
        hh = (1 - h) if a == 0 else h
        return span(hh * half + core * quarter, quarter)

    w_local = [pltpu.make_async_copy(w.at[w_rows(a, c), :], wv.at[a, :, cols], w_sem.at[a]) for a in range(2)]
    w_away = [rdma(w.at[w_rows(a, 1 - c), :], wv.at[a, :, cols], w_send.at[a], w_recv.at[a], partner) for a in range(2)]
    for a in range(2):
        w_away[a].start()
        w_local[a].start()

    def s_copy(chip, dy, b):
        src = saved.at[:, span(b * half + ys[dy] * block, block)]
        dst = sv.at[y, t, :, pl.ds(b * block, block)]
        if chip == 0 and dy == 0:
            return pltpu.make_async_copy(src, dst, s_recv.at[0, y, b])
        dev = along[dy] if chip == 0 else pair_along[dy]
        return rdma(src, dst, s_send.at[chip, dy, b], s_recv.at[chip, y, b], dev)

    def s_start(chip, dys):
        for dy in dys:
            for b in range(2):
                s_copy(chip, dy, b).start()

    s_start(0, range(NY))

    @pl.when(s < sections - 1)
    def _():
        s_start(1, (1, 2, 3))

    @pl.when(s < sections - 2)
    def _():
        s_start(1, (0,))

    def piece_rows(i):
        return span(i * rows, rows)

    def at(j):
        i, k = j // nk, j % nk
        return piece_rows(i), k * CW

    def x_copy(j):
        r, k = at(j)
        return rdma(gn.at[r, span(k, CW)], g.at[r, span(c * quarter + k, CW)], x_send.at[j], x_recv.at[j], up)

    def f_copy(j):
        r, k = at(j)
        here = g.at[r, span(c * quarter + k, CW)]
        return rdma(here, here, f_send.at[j], f_recv.at[j], partner)

    def p_copy(j):
        return rdma(ps.at[j], pr.at[j], p_send.at[j], p_recv.at[j], pair)

    def y_copy(i, side):
        r = piece_rows(i)
        dev = along[1] if side == 0 else along[NY - 1]
        return rdma(g.at[r, cols], gy.at[y, r, :], y_send.at[side, i], y_recv.at[side, i], dev)

    def y_keep(i):
        r = piece_rows(i)
        return pltpu.make_async_copy(g.at[r, cols], gy.at[y, r, :], yloc.at[i])

    def r_copy(i, side):
        here = gy.at[ys[NY - 1] if side == 0 else ys[1], piece_rows(i), pl.ds(side * block, block)]
        dev = along[1] if side == 0 else along[NY - 1]
        return rdma(here, here, r_send.at[side, i], r_recv.at[side, i], dev)

    def pass_on(i):
        for side in range(2):
            y_copy(i, side).wait_recv()
            r_copy(i, side).start()

    @pl.when(first)
    def _():
        here = pltpu.make_async_copy(og.at[:, my_half], g.at[own_rows, :], loc.at[0])
        here.start()
        g_pair.wait_recv()
        g_fwd.start()
        here.wait()
        g_partner.wait_recv()
        g_fwd.wait_recv()
        g_pair.wait_send()
        g_partner.wait_send()
        g_fwd.wait_send()

    def step(j, carry):
        i, k = j // nk, j % nk

        @pl.when(jnp.logical_and(j < total, jnp.logical_not(first)))
        def _():
            x_copy(j).wait_recv()
            f_copy(j).start()

        @pl.when(j >= SKEW)
        def _():
            f = j - SKEW
            r, kk = at(f)
            p_copy(f).wait_recv()
            summed = own[f] + pr[f].astype(F32) + g[r, span(c * quarter + kk, CW)].astype(F32)
            gn[r, span(kk, CW)] = summed.astype(BF16)

            @pl.when(s > 0)
            def _():
                x_copy(f).start()

        @pl.when(jnp.logical_and(j < total, k == nk - 1))
        def _():
            @pl.when(jnp.logical_not(first))
            def _():
                def forwarded(q, carry):
                    f_copy(i * nk + q).wait_recv()
                    return carry

                lax.fori_loop(0, nk, forwarded, 0)

            @pl.when(i == 0)
            def _():
                w_local[0].wait()
                w_away[0].wait_recv()

            def send_part(q, carry):
                f = i * nk + q
                ps[f] = nt_dot(g[piece_rows(i), :], wv[0, span(q * CW, CW), :]).astype(BF16)
                p_copy(f).start()
                return carry

            lax.fori_loop(0, nk, send_part, 0)
            for side in range(2):
                y_copy(i, side).start()
            y_keep(i).start()

            @pl.when(i == 0)
            def _():
                w_local[1].wait()
                w_away[1].wait_recv()

            @pl.when(i >= 2)
            def _():
                pass_on(i - 2)

        @pl.when(jnp.logical_and(j >= nk, j < total + nk))
        def _():
            f = j - nk
            r, kk = at(f)
            own[f] = nt_dot(g[r, :], wv[1, span(kk, CW), :])

        return carry

    lax.fori_loop(0, total + SKEW, step, 0)

    @pl.when(s == sections - 1)
    def _():
        s_start(1, (1, 2, 3))

    @pl.when(s >= sections - 2)
    def _():
        s_start(1, (0,))

    homes = [partner, pair, cross]
    blocks = [partner_t, pair_t, cross_t]
    home = [
        rdma(gn.at[span(b * rows, rows), :], out.at[:, t_cols], o_send.at[i], o_recv.at[i], dev)
        for i, (dev, b) in enumerate(zip(homes, blocks))
    ]
    for copy in home:
        copy.start()
    mine = pltpu.make_async_copy(gn.at[own_rows, :], out.at[:, t_cols], loc.at[0])
    mine.start()

    pass_on(2)
    pass_on(3)

    for chip in range(2):
        for yy in range(NY):
            for b in range(2):
                where = sv.at[yy, 0, :, pl.ds(b * block, block)]
                pltpu.make_async_copy(where, where, s_recv.at[chip, yy, b]).wait()
    tokens = [sv.at[:, c], sv.at[:, 2 + c]]
    across = [rdma(ref, ref, t_send.at[i], t_recv.at[i], partner) for i, ref in enumerate(tokens)]
    for copy in across:
        copy.start()
    for i in range(pieces):
        y_keep(i).wait()
        for side in range(2):
            r_copy(i, side).wait_recv()
    for copy in across:
        copy.wait_recv()

    def l_copy(k):
        return rdma(lo.at[k], lr.at[k], l_send.at[k], l_recv.at[k], level)

    def wgrad(b, k):
        left = sv[:, :, :, span(b * block, block)].reshape(NY * 4 * rows, block)
        right = gy[:, :, span(k * CW, CW)].reshape(NY * 4 * rows, CW)
        return tn_dot(left, right)

    def l_part(k, carry):
        lo[k] = wgrad(1 - l, k).astype(BF16)
        l_copy(k).start()
        return carry

    lax.fori_loop(0, nk, l_part, 0)

    def l_own(k, carry):
        wg[:, span(k * CW, CW)] = wgrad(l, k)
        return carry

    lax.fori_loop(0, nk, l_own, 0)

    def l_sum(k, carry):
        l_copy(k).wait_recv()
        wg[:, span(k * CW, CW)] = wg[:, span(k * CW, CW)] + lr[k].astype(F32)
        return carry

    lax.fori_loop(0, nk, l_sum, 0)

    mine.wait()
    for copy in home:
        copy.wait_recv()
        copy.wait_send()
    for copy in across:
        copy.wait_send()
    for a in range(2):
        w_away[a].wait_send()
    for i in range(pieces):
        for side in range(2):
            y_copy(i, side).wait_send()
            r_copy(i, side).wait_send()
    for chip in range(2):
        for dy in range(NY):
            for b in range(2):
                if chip or dy:
                    s_copy(chip, dy, b).wait_send()

    def drain(j, carry):
        p_copy(j).wait_send()

        @pl.when(s > 0)
        def _():
            x_copy(j).wait_send()

        @pl.when(jnp.logical_not(first))
        def _():
            f_copy(j).wait_send()

        return carry

    lax.fori_loop(0, total, drain, 0)

    def l_drain(k, carry):
        l_copy(k).wait_send()
        return carry

    lax.fori_loop(0, nk, l_drain, 0)


def on_device(saved, weight, out_grad):
    rows, width = out_grad.shape
    quarter, half = width // 4, width // 2
    nk = quarter // CW
    total = 4 * nk
    dma = pltpu.SemaphoreType.DMA
    vmem = pltpu.VMEM
    inside = pl.BlockSpec(memory_space=pltpu.VMEM)
    anywhere = pl.BlockSpec(memory_space=pl.ANY)
    own_input, weight_grad = pl.pallas_call(
        relay,
        out_shape=(
            jax.ShapeDtypeStruct((rows, width), BF16),
            jax.ShapeDtypeStruct((quarter // 2, quarter), F32),
        ),
        in_specs=[inside, anywhere, anywhere],
        out_specs=(inside, inside),
        scratch_shapes=[
            vmem((2, quarter, half), BF16),
            vmem((4 * rows, half), BF16),
            vmem((total, rows, CW), BF16),
            vmem((total, rows, CW), BF16),
            vmem((total, rows, CW), F32),
            vmem((4 * rows, quarter), BF16),
            vmem((NY, 4 * rows, quarter), BF16),
            vmem((NY, 4, rows, quarter), BF16),
            vmem((nk, quarter // 2, CW), BF16),
            vmem((nk, quarter // 2, CW), BF16),
            dma((2,)), dma((2,)), dma((2,)), dma((3,)), dma((3,)),
            dma((total,)), dma((total,)), dma((total,)), dma((total,)), dma((total,)), dma((total,)),
            dma((3,)), dma((3,)), dma((2, 4)), dma((2, 4)), dma((2, 4)), dma((2, 4)),
            dma((2, NY, 2)), dma((2, NY, 2)), dma((2,)), dma((2,)), dma((nk,)), dma((nk,)), dma((1,)), dma((4,)),
        ],
        compiler_params=pltpu.CompilerParams(
            collective_id=0, has_side_effects=True, vmem_limit_bytes=60 * 1024 * 1024
        ),
    )(out_grad, weight[0], saved[0])
    return (own_input[None], weight_grad[None])


def solution(mesh):
    placed = (
        P("section", ("dp", "tensor"), None),
        P("section", None, "tensor"),
        P(("dp", "tensor"), None),
    )
    return jax.shard_map(
        on_device,
        mesh=mesh,
        in_specs=placed,
        out_specs=(P("section", ("dp", "tensor"), None), P("section", "dp", "tensor")),
        check_vma=False,
    )
```

```python
import jax
import jax.numpy as jnp
from jax import lax
from jax.experimental import pallas as pl
from jax.experimental.pallas import tpu as pltpu
from jax.sharding import PartitionSpec as P

MESH = pl.DeviceIdType.MESH
BF16 = jnp.bfloat16
F32 = jnp.float32
CW = 256
NY = 4
SKEW = 7


def rdma(src, dst, send, recv, dev):
    return pltpu.make_async_remote_copy(
        src_ref=src, dst_ref=dst, send_sem=send, recv_sem=recv, device_id=dev, device_id_type=MESH
    )


def nt_dot(a, b):
    return lax.dot_general(a, b, (((1,), (1,)), ((), ())), preferred_element_type=F32)


def tn_dot(a, b):
    return lax.dot_general(a, b, (((0,), (0,)), ((), ())), preferred_element_type=F32)


def span(start, size):
    return pl.ds(pl.multiple_of(start, 128), size)


def relay(
    og, w, saved,
    out, wg,
    wv, g, ps, pr, own, gn, gy, sv, lo, lr,
    w_sem, w_send, w_recv, gi_send, gi_recv, gf_send, gf_recv, x_send, x_recv, f_send, f_recv, p_send, p_recv,
    o_send, o_recv, y_send, y_recv, r_send, r_recv, s_send, s_recv, t_send, t_recv, l_send, l_recv, loc, yloc,
):
    rows, width = og.shape
    quarter, half = width // 4, width // 2
    nk = quarter // CW
    pieces = 4
    total = pieces * nk
    block = quarter // 2
    sections = lax.axis_size("section")
    s, d, t = lax.axis_index("section"), lax.axis_index("dp"), lax.axis_index("tensor")
    l, y = d // NY, d % NY
    h, c = t // 2, t % 2
    partner_t = h * 2 + 1 - c
    pair_t = (1 - h) * 2 + c
    cross_t = (1 - h) * 2 + 1 - c
    pair_l = (1 - l) * NY
    partner = (s, d, partner_t)
    pair = (s, pair_l + y, pair_t)
    cross = (s, pair_l + y, cross_t)
    level = (s, pair_l + y, t)
    up = (lax.rem(s + sections - 1, sections), d, t)
    down = (lax.rem(s + 1, sections), d, t)
    first = s == sections - 1
    ys = [lax.rem(y + dy, NY) for dy in range(NY)]
    along = [(s, l * NY + ys[dy], t) for dy in range(NY)]
    pair_along = [(s, pair_l + ys[dy], pair_t) for dy in range(NY)]

    barrier = pltpu.get_barrier_semaphore()
    friends = [partner, pair, cross, level, up, down] + along[1:] + pair_along[1:]
    for dev in friends:
        pl.semaphore_signal(barrier, inc=1, device_id=dev, device_id_type=MESH)
    pl.semaphore_wait(barrier, len(friends))

    cols = span(c * quarter, quarter)
    t_cols = span(t * quarter, quarter)
    own_rows = span(t * rows, rows)
    pair_rows = span(pair_t * rows, rows)
    my_half = span(h * half, half)
    other_half = span((1 - h) * half, half)

    cuts = (0, half * 7 // 20, half * 14 // 20, half)

    def g_there(q):
        return pl.ds(cuts[q], cuts[q + 1] - cuts[q])

    def g_cols(q):
        return span((1 - h) * half + cuts[q], cuts[q + 1] - cuts[q])

    def g_fwd(q):
        here = g.at[pair_rows, g_there(q)]
        return rdma(here, here, gf_send.at[q], gf_recv.at[q], partner)

    g_pair = rdma(og.at[:, g_cols(0)], g.at[own_rows, g_there(0)], gi_send.at[0], gi_recv.at[0], pair)

    def g_lend(q):
        there = gn.at[pl.ds(0, rows), pl.ds(0, cuts[q + 1] - cuts[q])]
        return rdma(og.at[:, g_cols(q)], there, gf_send.at[q], gf_recv.at[q], pair)

    def g_relay(q, dev):
        here = gn.at[pl.ds(0, rows), pl.ds(0, cuts[q + 1] - cuts[q])]
        return rdma(here, g.at[pair_rows, g_there(q)], gi_send.at[q], gi_recv.at[q], dev)

    beside = [(1, s == sections - 2, down), (2, s == 0, up)]

    @pl.when(first)
    def _():
        g_pair.start()

    for q, lends, dev in beside:
        @pl.when(lends)
        def _():
            g_lend(q).start()

    g_partner = rdma(og.at[:, my_half], g.at[own_rows, :], gi_send.at[3], gi_recv.at[3], partner)

    @pl.when(first)
    def _():
        g_partner.start()

    def w_rows(a, core):
        hh = (1 - h) if a == 0 else h
        return span(hh * half + core * quarter, quarter)

    w_local = [pltpu.make_async_copy(w.at[w_rows(a, c), :], wv.at[a, :, cols], w_sem.at[a]) for a in range(2)]
    w_away = [rdma(w.at[w_rows(a, 1 - c), :], wv.at[a, :, cols], w_send.at[a], w_recv.at[a], partner) for a in range(2)]
    w_away[0].start()
    w_local[0].start()
    w_local[1].start()

    @pl.when(jnp.logical_not(first))
    def _():
        w_away[1].start()

    for q, lends, dev in beside:
        @pl.when(lends)
        def _():
            g_lend(q).wait_recv()
            g_relay(q, dev).start()

    def s_copy(chip, dy, b):
        src = saved.at[:, span(b * half + ys[dy] * block, block)]
        dst = sv.at[y, t, :, pl.ds(b * block, block)]
        if chip == 0 and dy == 0:
            return pltpu.make_async_copy(src, dst, s_recv.at[0, y, b])
        dev = along[dy] if chip == 0 else pair_along[dy]
        return rdma(src, dst, s_send.at[chip, dy, b], s_recv.at[chip, y, b], dev)

    def s_start(chip, dys):
        for dy in dys:
            for b in range(2):
                s_copy(chip, dy, b).start()

    s_start(0, range(NY))

    @pl.when(s < sections - 2)
    def _():
        s_start(1, range(NY))

    def piece_rows(i):
        return span(i * rows, rows)

    def at(j):
        i, k = j // nk, j % nk
        return piece_rows(i), k * CW

    def x_copy(j):
        r, k = at(j)
        return rdma(gn.at[r, span(k, CW)], g.at[r, span(c * quarter + k, CW)], x_send.at[j], x_recv.at[j], up)

    def f_copy(j):
        r, k = at(j)
        here = g.at[r, span(c * quarter + k, CW)]
        return rdma(here, here, f_send.at[j], f_recv.at[j], partner)

    def p_copy(j):
        return rdma(ps.at[j], pr.at[j], p_send.at[j], p_recv.at[j], pair)

    def y_copy(i, side):
        r = piece_rows(i)
        dev = along[1] if side == 0 else along[NY - 1]
        return rdma(g.at[r, cols], gy.at[y, r, :], y_send.at[side, i], y_recv.at[side, i], dev)

    def y_keep(i):
        r = piece_rows(i)
        return pltpu.make_async_copy(g.at[r, cols], gy.at[y, r, :], yloc.at[i])

    def r_copy(i, side):
        here = gy.at[ys[NY - 1] if side == 0 else ys[1], piece_rows(i), pl.ds(side * block, block)]
        dev = along[1] if side == 0 else along[NY - 1]
        return rdma(here, here, r_send.at[side, i], r_recv.at[side, i], dev)

    def pass_on(i):
        for side in range(2):
            y_copy(i, side).wait_recv()
            r_copy(i, side).start()

    @pl.when(first)
    def _():
        here = pltpu.make_async_copy(og.at[:, my_half], g.at[own_rows, :], loc.at[0])
        here.start()
        g_pair.wait_recv()
        g_fwd(0).start()
        for q, lends, dev in beside:
            g_relay(q, dev).wait_recv()
            g_fwd(q).start()
        w_away[1].start()
        here.wait()
        g_partner.wait_recv()
        g_partner.wait_send()
        g_pair.wait_send()
        for q in range(3):
            g_fwd(q).wait_recv()
            g_fwd(q).wait_send()

    for q, lends, dev in beside:
        @pl.when(lends)
        def _():
            g_lend(q).wait_send()
            g_relay(q, dev).wait_send()

    tokens = [sv.at[:, c], sv.at[:, 2 + c]]
    across = [rdma(ref, ref, t_send.at[i], t_recv.at[i], partner) for i, ref in enumerate(tokens)]

    def s_across():
        for chip in range(2):
            for yy in range(NY):
                for b in range(2):
                    where = sv.at[yy, 0, :, pl.ds(b * block, block)]
                    pltpu.make_async_copy(where, where, s_recv.at[chip, yy, b]).wait()
        for copy in across:
            copy.start()

    @pl.when(s == 0)
    def _():
        s_across()

    def step(j, carry):
        i, k = j // nk, j % nk

        @pl.when(jnp.logical_and(j < total, jnp.logical_not(first)))
        def _():
            x_copy(j).wait_recv()
            f_copy(j).start()

        @pl.when(j >= SKEW)
        def _():
            f = j - SKEW
            r, kk = at(f)
            p_copy(f).wait_recv()
            summed = own[f] + pr[f].astype(F32) + g[r, span(c * quarter + kk, CW)].astype(F32)
            gn[r, span(kk, CW)] = summed.astype(BF16)

            @pl.when(s > 0)
            def _():
                x_copy(f).start()

        @pl.when(jnp.logical_and(j < total, k == nk - 1))
        def _():
            for side in range(2):
                y_copy(i, side).start()
            y_keep(i).start()

            @pl.when(jnp.logical_not(first))
            def _():
                def forwarded(q, carry):
                    f_copy(i * nk + q).wait_recv()
                    return carry

                lax.fori_loop(0, nk, forwarded, 0)

            @pl.when(i == 0)
            def _():
                w_local[0].wait()
                w_away[0].wait_recv()

            def send_part(q, carry):
                f = i * nk + q
                ps[f] = nt_dot(g[piece_rows(i), :], wv[0, span(q * CW, CW), :]).astype(BF16)
                p_copy(f).start()
                return carry

            lax.fori_loop(0, nk, send_part, 0)

            @pl.when(i == 0)
            def _():
                w_local[1].wait()
                w_away[1].wait_recv()

            @pl.when(i >= 2)
            def _():
                pass_on(i - 2)

        @pl.when(j == total)
        def _():
            pass_on(2)

        @pl.when(j == total + 4)
        def _():
            pass_on(3)

        @pl.when(jnp.logical_and(j >= nk, j < total + nk))
        def _():
            f = j - nk
            r, kk = at(f)
            own[f] = nt_dot(g[r, :], wv[1, span(kk, CW), :])

        return carry

    lax.fori_loop(0, total + SKEW, step, 0)

    @pl.when(s >= sections - 2)
    def _():
        s_start(1, range(NY))

    homes = [partner, pair, cross]
    blocks = [partner_t, pair_t, cross_t]
    home = [
        rdma(gn.at[span(b * rows, rows), :], out.at[:, t_cols], o_send.at[i], o_recv.at[i], dev)
        for i, (dev, b) in enumerate(zip(homes, blocks))
    ]
    for copy in home:
        copy.start()
    mine = pltpu.make_async_copy(gn.at[own_rows, :], out.at[:, t_cols], loc.at[0])
    mine.start()


    @pl.when(s > 0)
    def _():
        s_across()

    for i in range(pieces):
        y_keep(i).wait()
        for side in range(2):
            r_copy(i, side).wait_recv()
    for copy in across:
        copy.wait_recv()

    def l_copy(k):
        return rdma(lo.at[k], lr.at[k], l_send.at[k], l_recv.at[k], level)

    def wgrad(b, k):
        left = sv[:, :, :, span(b * block, block)].reshape(NY * 4 * rows, block)
        right = gy[:, :, span(k * CW, CW)].reshape(NY * 4 * rows, CW)
        return tn_dot(left, right)

    def l_part(k, carry):
        lo[k] = wgrad(1 - l, k).astype(BF16)
        l_copy(k).start()
        return carry

    lax.fori_loop(0, nk, l_part, 0)

    def l_own(k, carry):
        wg[:, span(k * CW, CW)] = wgrad(l, k)
        return carry

    lax.fori_loop(0, nk, l_own, 0)

    def l_sum(k, carry):
        l_copy(k).wait_recv()
        wg[:, span(k * CW, CW)] = wg[:, span(k * CW, CW)] + lr[k].astype(F32)
        return carry

    lax.fori_loop(0, nk, l_sum, 0)

    mine.wait()
    for copy in home:
        copy.wait_recv()
        copy.wait_send()
    for copy in across:
        copy.wait_send()
    for a in range(2):
        w_away[a].wait_send()
    for i in range(pieces):
        for side in range(2):
            y_copy(i, side).wait_send()
            r_copy(i, side).wait_send()
    for chip in range(2):
        for dy in range(NY):
            for b in range(2):
                if chip or dy:
                    s_copy(chip, dy, b).wait_send()

    def drain(j, carry):
        p_copy(j).wait_send()

        @pl.when(s > 0)
        def _():
            x_copy(j).wait_send()

        @pl.when(jnp.logical_not(first))
        def _():
            f_copy(j).wait_send()

        return carry

    lax.fori_loop(0, total, drain, 0)

    def l_drain(k, carry):
        l_copy(k).wait_send()
        return carry

    lax.fori_loop(0, nk, l_drain, 0)


def on_device(saved, weight, out_grad):
    rows, width = out_grad.shape
    quarter, half = width // 4, width // 2
    nk = quarter // CW
    total = 4 * nk
    dma = pltpu.SemaphoreType.DMA
    vmem = pltpu.VMEM
    inside = pl.BlockSpec(memory_space=pltpu.VMEM)
    anywhere = pl.BlockSpec(memory_space=pl.ANY)
    own_input, weight_grad = pl.pallas_call(
        relay,
        out_shape=(
            jax.ShapeDtypeStruct((rows, width), BF16),
            jax.ShapeDtypeStruct((quarter // 2, quarter), F32),
        ),
        in_specs=[inside, anywhere, anywhere],
        out_specs=(inside, inside),
        scratch_shapes=[
            vmem((2, quarter, half), BF16),
            vmem((4 * rows, half), BF16),
            vmem((total, rows, CW), BF16),
            vmem((total, rows, CW), BF16),
            vmem((total, rows, CW), F32),
            vmem((4 * rows, quarter), BF16),
            vmem((NY, 4 * rows, quarter), BF16),
            vmem((NY, 4, rows, quarter), BF16),
            vmem((nk, quarter // 2, CW), BF16),
            vmem((nk, quarter // 2, CW), BF16),
            dma((2,)), dma((2,)), dma((2,)), dma((4,)), dma((4,)), dma((3,)), dma((3,)),
            dma((total,)), dma((total,)), dma((total,)), dma((total,)), dma((total,)), dma((total,)),
            dma((3,)), dma((3,)), dma((2, 4)), dma((2, 4)), dma((2, 4)), dma((2, 4)),
            dma((2, NY, 2)), dma((2, NY, 2)), dma((2,)), dma((2,)), dma((nk,)), dma((nk,)), dma((1,)), dma((4,)),
        ],
        compiler_params=pltpu.CompilerParams(
            collective_id=0, has_side_effects=True, vmem_limit_bytes=46 * 1024 * 1024
        ),
    )(out_grad, weight[0], saved[0])
    return (own_input[None], weight_grad[None])


def solution(mesh):
    placed = (
        P("section", ("dp", "tensor"), None),
        P("section", None, "tensor"),
        P(("dp", "tensor"), None),
    )
    return jax.shard_map(
        on_device,
        mesh=mesh,
        in_specs=placed,
        out_specs=(P("section", ("dp", "tensor"), None), P("section", "dp", "tensor")),
        check_vma=False,
    )
```

```python
import jax
import jax.numpy as jnp
from jax import lax
from jax.experimental import pallas as pl
from jax.experimental.pallas import tpu as pltpu
from jax.sharding import PartitionSpec as P

MESH = pl.DeviceIdType.MESH
BF16 = jnp.bfloat16
F32 = jnp.float32
CW = 256
NY = 4
SKEW = 7


def rdma(src, dst, send, recv, dev):
    return pltpu.make_async_remote_copy(
        src_ref=src, dst_ref=dst, send_sem=send, recv_sem=recv, device_id=dev, device_id_type=MESH
    )


def nt_dot(a, b):
    return lax.dot_general(a, b, (((1,), (1,)), ((), ())), preferred_element_type=F32)


def tn_dot(a, b):
    return lax.dot_general(a, b, (((0,), (0,)), ((), ())), preferred_element_type=F32)


def span(start, size):
    return pl.ds(pl.multiple_of(start, 128), size)


def relay(
    og, w, saved,
    out, wg,
    wv, g, ps, pr, own, gn, gy, sv, lo, lr, sv2, lo2, lr2,
    w_sem, w_send, w_recv, gi_send, gi_recv, gf_send, gf_recv, x_send, x_recv, f_send, f_recv, p_send, p_recv,
    o_send, o_recv, y_send, y_recv, r_send, r_recv, s_send, s_recv, t_send, t_recv, l_send, l_recv, loc, yloc,
    y2_send, y2_recv, g2_send, g2_recv, u_send, u_recv, v_send, v_recv, m_send, m_recv,
):
    rows, width = og.shape
    quarter, half = width // 4, width // 2
    nk = quarter // CW
    pieces = 4
    total = pieces * nk
    block = quarter // 2
    sections = lax.axis_size("section")
    s, d, t = lax.axis_index("section"), lax.axis_index("dp"), lax.axis_index("tensor")
    l, y = d // NY, d % NY
    h, c = t // 2, t % 2
    partner_t = h * 2 + 1 - c
    pair_t = (1 - h) * 2 + c
    cross_t = (1 - h) * 2 + 1 - c
    pair_l = (1 - l) * NY
    partner = (s, d, partner_t)
    pair = (s, pair_l + y, pair_t)
    cross = (s, pair_l + y, cross_t)
    level = (s, pair_l + y, t)
    up = (lax.rem(s + sections - 1, sections), d, t)
    down = (lax.rem(s + 1, sections), d, t)
    first = s == sections - 1
    ys = [lax.rem(y + dy, NY) for dy in range(NY)]
    along = [(s, l * NY + ys[dy], t) for dy in range(NY)]
    pair_along = [(s, pair_l + ys[dy], pair_t) for dy in range(NY)]

    barrier = pltpu.get_barrier_semaphore()
    friends = [partner, pair, cross, level, up, down] + along[1:] + pair_along[1:]
    for dev in friends:
        pl.semaphore_signal(barrier, inc=1, device_id=dev, device_id_type=MESH)
    pl.semaphore_wait(barrier, len(friends))

    cols = span(c * quarter, quarter)
    t_cols = span(t * quarter, quarter)
    own_rows = span(t * rows, rows)
    pair_rows = span(pair_t * rows, rows)
    my_half = span(h * half, half)
    other_half = span((1 - h) * half, half)

    cuts = (0, half * 7 // 20, half * 14 // 20, half)

    def g_there(q):
        return pl.ds(cuts[q], cuts[q + 1] - cuts[q])

    def g_cols(q):
        return span((1 - h) * half + cuts[q], cuts[q + 1] - cuts[q])

    def g_fwd(q):
        here = g.at[pair_rows, g_there(q)]
        return rdma(here, here, gf_send.at[q], gf_recv.at[q], partner)

    g_pair = rdma(og.at[:, g_cols(0)], g.at[own_rows, g_there(0)], gi_send.at[0], gi_recv.at[0], pair)

    def g_lend(q):
        there = gn.at[pl.ds(0, rows), pl.ds(0, cuts[q + 1] - cuts[q])]
        return rdma(og.at[:, g_cols(q)], there, gf_send.at[q], gf_recv.at[q], pair)

    def g_relay(q, dev):
        here = gn.at[pl.ds(0, rows), pl.ds(0, cuts[q + 1] - cuts[q])]
        return rdma(here, g.at[pair_rows, g_there(q)], gi_send.at[q], gi_recv.at[q], dev)

    beside = [(1, s == sections - 2, down), (2, s == 0, up)]

    @pl.when(first)
    def _():
        g_pair.start()

    for q, lends, dev in beside:
        @pl.when(lends)
        def _():
            g_lend(q).start()

    g_partner = rdma(og.at[:, my_half], g.at[own_rows, :], gi_send.at[3], gi_recv.at[3], partner)

    @pl.when(first)
    def _():
        g_partner.start()

    def w_rows(a, core):
        hh = (1 - h) if a == 0 else h
        return span(hh * half + core * quarter, quarter)

    w_local = [pltpu.make_async_copy(w.at[w_rows(a, c), :], wv.at[a, :, cols], w_sem.at[a]) for a in range(2)]
    w_away = [rdma(w.at[w_rows(a, 1 - c), :], wv.at[a, :, cols], w_send.at[a], w_recv.at[a], partner) for a in range(2)]
    w_away[0].start()
    w_local[0].start()
    w_local[1].start()

    @pl.when(jnp.logical_not(first))
    def _():
        w_away[1].start()

    for q, lends, dev in beside:
        @pl.when(lends)
        def _():
            g_lend(q).wait_recv()
            g_relay(q, dev).start()

    def s_copy(chip, dy, b):
        src = saved.at[:, span(b * half + ys[dy] * block, block)]
        dst = sv.at[y, t, :, pl.ds(b * block, block)]
        if chip == 0 and dy == 0:
            return pltpu.make_async_copy(src, dst, s_recv.at[0, y, b])
        dev = along[dy] if chip == 0 else pair_along[dy]
        return rdma(src, dst, s_send.at[chip, dy, b], s_recv.at[chip, y, b], dev)

    def s_start(chip, dys):
        for dy in dys:
            for b in range(2):
                s_copy(chip, dy, b).start()

    s_start(0, range(NY))

    @pl.when(s < sections - 1)
    def _():
        s_start(1, (1, 2))

    @pl.when(s < sections - 2)
    def _():
        s_start(1, (0, 3))

    def piece_rows(i):
        return span(i * rows, rows)

    def at(j):
        i, k = j // nk, j % nk
        return piece_rows(i), k * CW

    def x_copy(j):
        r, k = at(j)
        return rdma(gn.at[r, span(k, CW)], g.at[r, span(c * quarter + k, CW)], x_send.at[j], x_recv.at[j], up)

    def f_copy(j):
        r, k = at(j)
        here = g.at[r, span(c * quarter + k, CW)]
        return rdma(here, here, f_send.at[j], f_recv.at[j], partner)

    def p_copy(j):
        return rdma(ps.at[j], pr.at[j], p_send.at[j], p_recv.at[j], pair)

    def y_copy(i, side):
        r = piece_rows(i)
        dev = along[1] if side == 0 else along[NY - 1]
        return rdma(g.at[r, cols], gy.at[y, r, :], y_send.at[side, i], y_recv.at[side, i], dev)

    def y_keep(i):
        r = piece_rows(i)
        return pltpu.make_async_copy(g.at[r, cols], gy.at[y, r, :], yloc.at[i])

    def r_copy(i, side):
        here = gy.at[ys[NY - 1] if side == 0 else ys[1], piece_rows(i), pl.ds(side * block, block)]
        dev = along[1] if side == 0 else along[NY - 1]
        return rdma(here, here, r_send.at[side, i], r_recv.at[side, i], dev)

    last = s == 0
    l_half = span(c * quarter + l * block, block)
    near, far = pl.ds(0, block), pl.ds(block, block)

    def g2_copy(i):
        r = piece_rows(i)
        return rdma(
            g.at[r, span(c * quarter + (1 - l) * block, block)], gy.at[y, r, far], g2_send.at[i], g2_recv.at[i], level
        )

    def y0_copy(i, side):
        r = piece_rows(i)
        dev = along[1] if side == 0 else along[NY - 1]
        return rdma(g.at[r, l_half], gy.at[y, r, near], y_send.at[side, i], y_recv.at[side, i], dev)

    def y2_copy(i, side):
        here = gy.at[y, piece_rows(i), far]
        dev = along[1] if side == 0 else along[NY - 1]
        return rdma(here, here, y2_send.at[side, i], y2_recv.at[side, i], dev)

    def y0_keep(i):
        r = piece_rows(i)
        return pltpu.make_async_copy(g.at[r, l_half], gy.at[y, r, near], yloc.at[i])

    def spread(i):
        @pl.when(last)
        def _():
            g2_copy(i).start()
            for side in range(2):
                y0_copy(i, side).start()
            y0_keep(i).start()

        @pl.when(jnp.logical_not(last))
        def _():
            for side in range(2):
                y_copy(i, side).start()
            y_keep(i).start()

    def spread_far(i):
        g2_copy(i).wait_recv()
        for side in range(2):
            y2_copy(i, side).start()

    def pass_near(i):
        y0_copy(i, 0).wait_recv()
        r_copy(i, 0).start()

    def pass_far(i):
        y2_copy(i, 1).wait_recv()
        r_copy(i, 1).start()

    def pass_on(i):
        for side in range(2):
            y_copy(i, side).wait_recv()
            r_copy(i, side).start()

    @pl.when(first)
    def _():
        here = pltpu.make_async_copy(og.at[:, my_half], g.at[own_rows, :], loc.at[0])
        here.start()
        g_pair.wait_recv()
        g_fwd(0).start()
        for q, lends, dev in beside:
            g_relay(q, dev).wait_recv()
            g_fwd(q).start()
        w_away[1].start()
        here.wait()
        g_partner.wait_recv()
        g_partner.wait_send()
        g_pair.wait_send()
        for q in range(3):
            g_fwd(q).wait_recv()
            g_fwd(q).wait_send()

    for q, lends, dev in beside:
        @pl.when(lends)
        def _():
            g_lend(q).wait_send()
            g_relay(q, dev).wait_send()

    tokens = [sv.at[:, c], sv.at[:, 2 + c]]
    across = [rdma(ref, ref, t_send.at[i], t_recv.at[i], partner) for i, ref in enumerate(tokens)]

    def s_arrived(chip):
        for yy in range(NY):
            for b in range(2):
                where = sv.at[yy, 0, :, pl.ds(b * block, block)]
                pltpu.make_async_copy(where, where, s_recv.at[chip, yy, b]).wait()

    def s_across():
        for copy in across:
            copy.start()

    beyond = [(sv.at[:, t], sv2.at[:, t]), (sv.at[:, pair_t], sv2.at[:, pair_t])]
    lent = [rdma(*beyond[0], u_send.at[0], u_recv.at[0], level)] + [
        rdma(sv.at[yy, pair_t], sv2.at[yy, pair_t], u_send.at[1 + yy], u_recv.at[1 + yy], level) for yy in range(NY)
    ]
    across2 = [rdma(dst, dst, v_send.at[i], v_recv.at[i], partner) for i, (src, dst) in enumerate(beyond)]

    @pl.when(last)
    def _():
        s_arrived(0)
        lent[0].start()
        s_arrived(1)
        lent[1].start()
        lent[2].start()
        s_across()

    def step(j, carry):
        i, k = j // nk, j % nk

        @pl.when(jnp.logical_and(j < total, jnp.logical_not(first)))
        def _():
            x_copy(j).wait_recv()
            f_copy(j).start()

        @pl.when(j >= SKEW)
        def _():
            f = j - SKEW
            r, kk = at(f)
            p_copy(f).wait_recv()
            summed = own[f] + pr[f].astype(F32) + g[r, span(c * quarter + kk, CW)].astype(F32)
            gn[r, span(kk, CW)] = summed.astype(BF16)

            @pl.when(s > 0)
            def _():
                x_copy(f).start()

        @pl.when(jnp.logical_and(j < total, k == nk - 1))
        def _():
            spread(i)
            for q in range(2):
                @pl.when(jnp.logical_and(last, i == q))
                def _():
                    lent[3 + q].start()

            @pl.when(jnp.logical_and(last, i > 0))
            def _():
                pass_near(i - 1)

            @pl.when(jnp.logical_not(first))
            def _():
                def forwarded(q, carry):
                    f_copy(i * nk + q).wait_recv()
                    return carry

                lax.fori_loop(0, nk, forwarded, 0)

            @pl.when(i == 0)
            def _():
                w_local[0].wait()
                w_away[0].wait_recv()

            def send_part(q, carry):
                f = i * nk + q
                ps[f] = nt_dot(g[piece_rows(i), :], wv[0, span(q * CW, CW), :]).astype(BF16)
                p_copy(f).start()
                return carry

            lax.fori_loop(0, nk, send_part, 0)

            @pl.when(i == 0)
            def _():
                w_local[1].wait()
                w_away[1].wait_recv()

            @pl.when(jnp.logical_and(last, i == 3))
            def _():
                for copy in lent:
                    copy.wait_recv()
                for on in across2:
                    on.start()

            @pl.when(jnp.logical_and(jnp.logical_not(last), i >= 2))
            def _():
                pass_on(i - 2)

        @pl.when(jnp.logical_and(last, jnp.logical_and(j < total, k == nk - 2)))
        def _():
            @pl.when(i >= 1)
            def _():
                spread_far(i - 1)

            @pl.when(i >= 2)
            def _():
                pass_far(i - 2)

        @pl.when(j == total)
        def _():
            @pl.when(last)
            def _():
                spread_far(pieces - 1)
                pass_far(pieces - 2)
                pass_near(pieces - 1)

            @pl.when(jnp.logical_not(last))
            def _():
                pass_on(pieces - 2)

        @pl.when(j == total + 4)
        def _():
            @pl.when(last)
            def _():
                pass_far(pieces - 1)

            @pl.when(jnp.logical_not(last))
            def _():
                pass_on(pieces - 1)

        @pl.when(jnp.logical_and(j >= nk, j < total + nk))
        def _():
            f = j - nk
            r, kk = at(f)
            own[f] = nt_dot(g[r, :], wv[1, span(kk, CW), :])

        return carry

    lax.fori_loop(0, total + SKEW, step, 0)

    @pl.when(s == sections - 1)
    def _():
        s_start(1, (1, 2))

    @pl.when(s >= sections - 2)
    def _():
        s_start(1, (0, 3))

    homes = [partner, pair, cross]
    blocks = [partner_t, pair_t, cross_t]
    home = [
        rdma(gn.at[span(b * rows, rows), :], out.at[:, t_cols], o_send.at[i], o_recv.at[i], dev)
        for i, (dev, b) in enumerate(zip(homes, blocks))
    ]
    for copy in home:
        copy.start()
    mine = pltpu.make_async_copy(gn.at[own_rows, :], out.at[:, t_cols], loc.at[0])
    mine.start()


    @pl.when(s > 0)
    def _():
        for chip in range(2):
            s_arrived(chip)
        s_across()

    @pl.when(last)
    def _():
        for i in range(pieces):
            y0_keep(i).wait()
            y0_copy(i, 1).wait_recv()
            y2_copy(i, 0).wait_recv()
        for on in across2:
            on.wait_recv()

    @pl.when(jnp.logical_not(last))
    def _():
        for i in range(pieces):
            y_keep(i).wait()

    for i in range(pieces):
        for side in range(2):
            r_copy(i, side).wait_recv()
    for copy in across:
        copy.wait_recv()

    def l_copy(k):
        return rdma(lo.at[k], lr.at[k], l_send.at[k], l_recv.at[k], level)

    def wgrad(b, k):
        left = sv[:, :, :, span(b * block, block)].reshape(NY * 4 * rows, block)
        right = gy[:, :, span(k * CW, CW)].reshape(NY * 4 * rows, CW)
        return tn_dot(left, right)

    def l_part(k, carry):
        lo[k] = wgrad(1 - l, k).astype(BF16)
        l_copy(k).start()
        return carry

    def l_own(k, carry):
        wg[:, span(k * CW, CW)] = wgrad(l, k)
        return carry

    def l_sum(k, carry):
        l_copy(k).wait_recv()
        wg[:, span(k * CW, CW)] = wg[:, span(k * CW, CW)] + lr[k].astype(F32)
        return carry

    parts = ((0, 128), (128, 256), (384, 256))

    def m_copy(k):
        here = pl.ds(*parts[k])
        return rdma(lo2.at[:, here], lr2.at[:, here], m_send.at[k], m_recv.at[k], level)

    def both(b, k):
        at, wide = parts[k]

        def part(ref, start):
            left = ref[:, :, :, span(b * block, block)].reshape(NY * 4 * rows, block)
            return tn_dot(left, gy[:, :, pl.ds(start + at, wide)].reshape(NY * 4 * rows, wide))

        return part(sv, 0) + part(sv2, block)

    def m_all():
        for k, (at, wide) in enumerate(parts):
            lo2[:, pl.ds(at, wide)] = both(1 - l, k).astype(BF16)
            m_copy(k).start()
        for k, (at, wide) in enumerate(parts):
            wg[:, span(l * block + at, wide)] = both(l, k)
        for k, (at, wide) in enumerate(parts):
            m_copy(k).wait_recv()
            wg[:, span((1 - l) * block + at, wide)] = lr2[:, pl.ds(at, wide)].astype(F32)

    @pl.when(last)
    def _():
        m_all()

    @pl.when(jnp.logical_not(last))
    def _():
        lax.fori_loop(0, nk, l_part, 0)
        lax.fori_loop(0, nk, l_own, 0)
        lax.fori_loop(0, nk, l_sum, 0)

    mine.wait()
    for copy in home:
        copy.wait_recv()
        copy.wait_send()
    for copy in across:
        copy.wait_send()
    for a in range(2):
        w_away[a].wait_send()
    for i in range(pieces):
        for side in range(2):
            r_copy(i, side).wait_send()

    @pl.when(last)
    def _():
        for i in range(pieces):
            g2_copy(i).wait_send()
            for side in range(2):
                y0_copy(i, side).wait_send()
                y2_copy(i, side).wait_send()
        for copy in lent + across2:
            copy.wait_send()
        for k in range(len(parts)):
            m_copy(k).wait_send()

    @pl.when(jnp.logical_not(last))
    def _():
        for i in range(pieces):
            for side in range(2):
                y_copy(i, side).wait_send()
        for k in range(nk):
            l_copy(k).wait_send()
    for chip in range(2):
        for dy in range(NY):
            for b in range(2):
                if chip or dy:
                    s_copy(chip, dy, b).wait_send()

    def drain(j, carry):
        p_copy(j).wait_send()

        @pl.when(s > 0)
        def _():
            x_copy(j).wait_send()

        @pl.when(jnp.logical_not(first))
        def _():
            f_copy(j).wait_send()

        return carry

    lax.fori_loop(0, total, drain, 0)


def on_device(saved, weight, out_grad):
    rows, width = out_grad.shape
    quarter, half = width // 4, width // 2
    nk = quarter // CW
    total = 4 * nk
    dma = pltpu.SemaphoreType.DMA
    vmem = pltpu.VMEM
    inside = pl.BlockSpec(memory_space=pltpu.VMEM)
    anywhere = pl.BlockSpec(memory_space=pl.ANY)
    own_input, weight_grad = pl.pallas_call(
        relay,
        out_shape=(
            jax.ShapeDtypeStruct((rows, width), BF16),
            jax.ShapeDtypeStruct((quarter // 2, quarter), F32),
        ),
        in_specs=[inside, anywhere, anywhere],
        out_specs=(inside, inside),
        scratch_shapes=[
            vmem((2, quarter, half), BF16),
            vmem((4 * rows, half), BF16),
            vmem((total, rows, CW), BF16),
            vmem((total, rows, CW), BF16),
            vmem((total, rows, CW), F32),
            vmem((4 * rows, quarter), BF16),
            vmem((NY, 4 * rows, quarter), BF16),
            vmem((NY, 4, rows, quarter), BF16),
            vmem((nk, quarter // 2, CW), BF16),
            vmem((nk, quarter // 2, CW), BF16),
            vmem((NY, 4, rows, quarter), BF16),
            vmem((quarter // 2, quarter // 2), BF16),
            vmem((quarter // 2, quarter // 2), BF16),
            dma((2,)), dma((2,)), dma((2,)), dma((4,)), dma((4,)), dma((3,)), dma((3,)),
            dma((total,)), dma((total,)), dma((total,)), dma((total,)), dma((total,)), dma((total,)),
            dma((3,)), dma((3,)), dma((2, 4)), dma((2, 4)), dma((2, 4)), dma((2, 4)),
            dma((2, NY, 2)), dma((2, NY, 2)), dma((2,)), dma((2,)), dma((nk,)), dma((nk,)), dma((1,)), dma((4,)),
            dma((2, 4)), dma((2, 4)), dma((4,)), dma((4,)), dma((5,)), dma((5,)), dma((2,)), dma((2,)),
            dma((3,)), dma((3,)),
        ],
        compiler_params=pltpu.CompilerParams(
            collective_id=0, has_side_effects=True, vmem_limit_bytes=50 * 1024 * 1024
        ),
    )(out_grad, weight[0], saved[0])
    return (own_input[None], weight_grad[None])


def solution(mesh):
    placed = (
        P("section", ("dp", "tensor"), None),
        P("section", None, "tensor"),
        P(("dp", "tensor"), None),
    )
    return jax.shard_map(
        on_device,
        mesh=mesh,
        in_specs=placed,
        out_specs=(P("section", ("dp", "tensor"), None), P("section", "dp", "tensor")),
        check_vma=False,
    )
```

```python
import jax
import jax.numpy as jnp
from jax import lax
from jax.experimental import pallas as pl
from jax.experimental.pallas import tpu as pltpu
from jax.sharding import PartitionSpec as P

MESH = pl.DeviceIdType.MESH
BF16 = jnp.bfloat16
F32 = jnp.float32
CW = 256
NY = 4
SKEW = 7


def rdma(src, dst, send, recv, dev):
    return pltpu.make_async_remote_copy(
        src_ref=src, dst_ref=dst, send_sem=send, recv_sem=recv, device_id=dev, device_id_type=MESH
    )


def nt_dot(a, b):
    return lax.dot_general(a, b, (((1,), (1,)), ((), ())), preferred_element_type=F32)


def tn_dot(a, b):
    return lax.dot_general(a, b, (((0,), (0,)), ((), ())), preferred_element_type=F32)


def span(start, size):
    return pl.ds(pl.multiple_of(start, 128), size)


def relay(
    og, w, saved,
    out, wg,
    wv, g, ps, pr, own, gn, gy, sv, lo, lr, sv2, lo2, lr2,
    w_sem, w_send, w_recv, gi_send, gi_recv, gf_send, gf_recv, x_send, x_recv, f_send, f_recv, p_send, p_recv,
    o_send, o_recv, y_send, y_recv, r_send, r_recv, s_send, s_recv, t_send, t_recv, l_send, l_recv, loc, yloc,
    y2_send, y2_recv, g2_send, g2_recv, u_send, u_recv, v_send, v_recv, m_send, m_recv,
):
    rows, width = og.shape
    quarter, half = width // 4, width // 2
    nk = quarter // CW
    pieces = 4
    total = pieces * nk
    block = quarter // 2
    sections = lax.axis_size("section")
    s, d, t = lax.axis_index("section"), lax.axis_index("dp"), lax.axis_index("tensor")
    l, y = d // NY, d % NY
    h, c = t // 2, t % 2
    partner_t = h * 2 + 1 - c
    pair_t = (1 - h) * 2 + c
    cross_t = (1 - h) * 2 + 1 - c
    pair_l = (1 - l) * NY
    partner = (s, d, partner_t)
    pair = (s, pair_l + y, pair_t)
    cross = (s, pair_l + y, cross_t)
    level = (s, pair_l + y, t)
    up = (lax.rem(s + sections - 1, sections), d, t)
    down = (lax.rem(s + 1, sections), d, t)
    first = s == sections - 1
    ys = [lax.rem(y + dy, NY) for dy in range(NY)]
    along = [(s, l * NY + ys[dy], t) for dy in range(NY)]
    pair_along = [(s, pair_l + ys[dy], pair_t) for dy in range(NY)]

    barrier = pltpu.get_barrier_semaphore()
    friends = [partner, pair, cross, level, up, down] + along[1:] + pair_along[1:]
    for dev in friends:
        pl.semaphore_signal(barrier, inc=1, device_id=dev, device_id_type=MESH)
    pl.semaphore_wait(barrier, len(friends))

    cols = span(c * quarter, quarter)
    t_cols = span(t * quarter, quarter)
    own_rows = span(t * rows, rows)
    pair_rows = span(pair_t * rows, rows)
    my_half = span(h * half, half)
    other_half = span((1 - h) * half, half)

    cuts = (0, half * 7 // 20, half * 14 // 20, half)

    def g_there(q):
        return pl.ds(cuts[q], cuts[q + 1] - cuts[q])

    def g_cols(q):
        return span((1 - h) * half + cuts[q], cuts[q + 1] - cuts[q])

    def g_fwd(q):
        here = g.at[pair_rows, g_there(q)]
        return rdma(here, here, gf_send.at[q], gf_recv.at[q], partner)

    g_pair = rdma(og.at[:, g_cols(0)], g.at[own_rows, g_there(0)], gi_send.at[0], gi_recv.at[0], pair)

    def g_lend(q):
        there = gn.at[pl.ds(0, rows), pl.ds(0, cuts[q + 1] - cuts[q])]
        return rdma(og.at[:, g_cols(q)], there, gf_send.at[q], gf_recv.at[q], pair)

    def g_relay(q, dev):
        here = gn.at[pl.ds(0, rows), pl.ds(0, cuts[q + 1] - cuts[q])]
        return rdma(here, g.at[pair_rows, g_there(q)], gi_send.at[q], gi_recv.at[q], dev)

    beside = [(1, s == sections - 2, down), (2, s == 0, up)]

    @pl.when(first)
    def _():
        g_pair.start()

    for q, lends, dev in beside:
        @pl.when(lends)
        def _():
            g_lend(q).start()

    g_partner = rdma(og.at[:, my_half], g.at[own_rows, :], gi_send.at[3], gi_recv.at[3], partner)

    @pl.when(first)
    def _():
        g_partner.start()

    def w_rows(a, core):
        hh = (1 - h) if a == 0 else h
        return span(hh * half + core * quarter, quarter)

    w_local = [pltpu.make_async_copy(w.at[w_rows(a, c), :], wv.at[a, :, cols], w_sem.at[a]) for a in range(2)]
    w_away = [rdma(w.at[w_rows(a, 1 - c), :], wv.at[a, :, cols], w_send.at[a], w_recv.at[a], partner) for a in range(2)]
    w_away[0].start()
    w_local[0].start()
    w_local[1].start()

    @pl.when(jnp.logical_not(first))
    def _():
        w_away[1].start()

    for q, lends, dev in beside:
        @pl.when(lends)
        def _():
            g_lend(q).wait_recv()
            g_relay(q, dev).start()

    def s_copy(chip, dy, b):
        src = saved.at[:, span(b * half + ys[dy] * block, block)]
        dst = sv.at[y, t, :, pl.ds(b * block, block)]
        if chip == 0 and dy == 0:
            return pltpu.make_async_copy(src, dst, s_recv.at[0, y, b])
        dev = along[dy] if chip == 0 else pair_along[dy]
        return rdma(src, dst, s_send.at[chip, dy, b], s_recv.at[chip, y, b], dev)

    def s_start(chip, dys):
        for dy in dys:
            for b in range(2):
                s_copy(chip, dy, b).start()

    s_start(0, range(NY))

    @pl.when(s < sections - 1)
    def _():
        s_start(1, (1, 2))

    @pl.when(s < sections - 2)
    def _():
        s_start(1, (0, 3))

    def piece_rows(i):
        return span(i * rows, rows)

    def at(j):
        i, k = j // nk, j % nk
        return piece_rows(i), k * CW

    def x_copy(j):
        r, k = at(j)
        return rdma(gn.at[r, span(k, CW)], g.at[r, span(c * quarter + k, CW)], x_send.at[j], x_recv.at[j], up)

    def f_copy(j):
        r, k = at(j)
        here = g.at[r, span(c * quarter + k, CW)]
        return rdma(here, here, f_send.at[j], f_recv.at[j], partner)

    def p_copy(j):
        return rdma(ps.at[j], pr.at[j], p_send.at[j], p_recv.at[j], pair)

    def y_copy(i, side):
        r = piece_rows(i)
        dev = along[1] if side == 0 else along[NY - 1]
        return rdma(g.at[r, cols], gy.at[y, r, :], y_send.at[side, i], y_recv.at[side, i], dev)

    def y_keep(i):
        r = piece_rows(i)
        return pltpu.make_async_copy(g.at[r, cols], gy.at[y, r, :], yloc.at[i])

    def r_copy(i, side):
        here = gy.at[ys[NY - 1] if side == 0 else ys[1], piece_rows(i), pl.ds(side * block, block)]
        dev = along[1] if side == 0 else along[NY - 1]
        return rdma(here, here, r_send.at[side, i], r_recv.at[side, i], dev)

    last = s == 0
    l_half = span(c * quarter + l * block, block)
    near, far = pl.ds(0, block), pl.ds(block, block)

    def g2_copy(i):
        r = piece_rows(i)
        return rdma(
            g.at[r, span(c * quarter + (1 - l) * block, block)], gy.at[y, r, far], g2_send.at[i], g2_recv.at[i], level
        )

    def y0_copy(i, side):
        r = piece_rows(i)
        dev = along[1] if side == 0 else along[NY - 1]
        return rdma(g.at[r, l_half], gy.at[y, r, near], y_send.at[side, i], y_recv.at[side, i], dev)

    def y2_copy(i, side):
        here = gy.at[y, piece_rows(i), far]
        dev = along[1] if side == 0 else along[NY - 1]
        return rdma(here, here, y2_send.at[side, i], y2_recv.at[side, i], dev)

    def y0_keep(i):
        r = piece_rows(i)
        return pltpu.make_async_copy(g.at[r, l_half], gy.at[y, r, near], yloc.at[i])

    def spread(i):
        @pl.when(last)
        def _():
            g2_copy(i).start()
            for side in range(2):
                y0_copy(i, side).start()
            y0_keep(i).start()

        @pl.when(jnp.logical_not(last))
        def _():
            for side in range(2):
                y_copy(i, side).start()
            y_keep(i).start()

    def spread_far(i):
        g2_copy(i).wait_recv()
        for side in range(2):
            y2_copy(i, side).start()

    def pass_near(i):
        y0_copy(i, 0).wait_recv()
        r_copy(i, 0).start()

    def pass_far(i):
        y2_copy(i, 1).wait_recv()
        r_copy(i, 1).start()

    def pass_on(i):
        for side in range(2):
            y_copy(i, side).wait_recv()
            r_copy(i, side).start()

    @pl.when(first)
    def _():
        here = pltpu.make_async_copy(og.at[:, my_half], g.at[own_rows, :], loc.at[0])
        here.start()
        g_pair.wait_recv()
        g_fwd(0).start()
        for q, lends, dev in beside:
            g_relay(q, dev).wait_recv()
            g_fwd(q).start()
        w_away[1].start()
        here.wait()
        g_partner.wait_recv()
        g_partner.wait_send()
        g_pair.wait_send()
        for q in range(3):
            g_fwd(q).wait_recv()
            g_fwd(q).wait_send()

    for q, lends, dev in beside:
        @pl.when(lends)
        def _():
            g_lend(q).wait_send()
            g_relay(q, dev).wait_send()

    tokens = [sv.at[:, c], sv.at[:, 2 + c]]
    across = [rdma(ref, ref, t_send.at[i], t_recv.at[i], partner) for i, ref in enumerate(tokens)]

    def s_arrived(chip):
        for yy in range(NY):
            for b in range(2):
                where = sv.at[yy, 0, :, pl.ds(b * block, block)]
                pltpu.make_async_copy(where, where, s_recv.at[chip, yy, b]).wait()

    def s_across():
        for copy in across:
            copy.start()

    beyond = [(sv.at[:, t], sv2.at[:, t]), (sv.at[:, pair_t], sv2.at[:, pair_t])]
    lent = [rdma(*beyond[0], u_send.at[0], u_recv.at[0], level)] + [
        rdma(sv.at[yy, pair_t], sv2.at[yy, pair_t], u_send.at[1 + yy], u_recv.at[1 + yy], level) for yy in range(NY)
    ]
    across2 = [rdma(dst, dst, v_send.at[i], v_recv.at[i], partner) for i, (src, dst) in enumerate(beyond)]

    @pl.when(last)
    def _():
        s_arrived(0)
        lent[0].start()
        s_arrived(1)
        lent[1].start()
        lent[2].start()
        s_across()

    def step(j, carry):
        i, k = j // nk, j % nk

        @pl.when(jnp.logical_and(j < total, jnp.logical_not(first)))
        def _():
            x_copy(j).wait_recv()
            f_copy(j).start()

        @pl.when(j >= SKEW)
        def _():
            f = j - SKEW
            r, kk = at(f)
            p_copy(f).wait_recv()
            summed = own[f] + pr[f].astype(F32) + g[r, span(c * quarter + kk, CW)].astype(F32)
            gn[r, span(kk, CW)] = summed.astype(BF16)

            @pl.when(s > 0)
            def _():
                x_copy(f).start()

        @pl.when(jnp.logical_and(j < total, k == nk - 1))
        def _():
            spread(i)
            for q in range(2):
                @pl.when(jnp.logical_and(last, i == q))
                def _():
                    lent[3 + q].start()

            @pl.when(jnp.logical_and(last, i > 0))
            def _():
                pass_near(i - 1)

            @pl.when(jnp.logical_not(first))
            def _():
                def forwarded(q, carry):
                    f_copy(i * nk + q).wait_recv()
                    return carry

                lax.fori_loop(0, nk, forwarded, 0)

            @pl.when(i == 0)
            def _():
                w_local[0].wait()
                w_away[0].wait_recv()

            def send_part(q, carry):
                f = i * nk + q
                ps[f] = nt_dot(g[piece_rows(i), :], wv[0, span(q * CW, CW), :]).astype(BF16)
                p_copy(f).start()
                return carry

            lax.fori_loop(0, nk, send_part, 0)

            @pl.when(i == 0)
            def _():
                w_local[1].wait()
                w_away[1].wait_recv()

            @pl.when(jnp.logical_and(last, i == 3))
            def _():
                for copy in lent:
                    copy.wait_recv()
                for on in across2:
                    on.start()

            @pl.when(jnp.logical_and(jnp.logical_not(last), i >= 2))
            def _():
                pass_on(i - 2)

        @pl.when(jnp.logical_and(last, jnp.logical_and(j < total, k == nk - 2)))
        def _():
            @pl.when(i >= 1)
            def _():
                spread_far(i - 1)

            @pl.when(i >= 2)
            def _():
                pass_far(i - 2)

        @pl.when(j == total)
        def _():
            @pl.when(last)
            def _():
                spread_far(pieces - 1)
                pass_far(pieces - 2)
                pass_near(pieces - 1)

            @pl.when(jnp.logical_not(last))
            def _():
                pass_on(pieces - 2)

        @pl.when(j == total + 4)
        def _():
            @pl.when(last)
            def _():
                pass_far(pieces - 1)

            @pl.when(jnp.logical_not(last))
            def _():
                pass_on(pieces - 1)

        @pl.when(jnp.logical_and(j >= nk, j < total + nk))
        def _():
            f = j - nk
            r, kk = at(f)
            own[f] = nt_dot(g[r, :], wv[1, span(kk, CW), :])

        return carry

    lax.fori_loop(0, total + SKEW, step, 0)

    @pl.when(s == sections - 1)
    def _():
        s_start(1, (1, 2))

    @pl.when(s >= sections - 2)
    def _():
        s_start(1, (0, 3))

    homes = [partner, pair, cross]
    blocks = [partner_t, pair_t, cross_t]
    home = [
        rdma(gn.at[span(b * rows, rows), :], out.at[:, t_cols], o_send.at[i], o_recv.at[i], dev)
        for i, (dev, b) in enumerate(zip(homes, blocks))
    ]
    for copy in home:
        copy.start()
    mine = pltpu.make_async_copy(gn.at[own_rows, :], out.at[:, t_cols], loc.at[0])
    mine.start()


    @pl.when(s > 0)
    def _():
        for chip in range(2):
            s_arrived(chip)
        s_across()

    @pl.when(last)
    def _():
        for i in range(pieces):
            y0_keep(i).wait()
            y0_copy(i, 1).wait_recv()
            y2_copy(i, 0).wait_recv()
        for on in across2:
            on.wait_recv()

    @pl.when(jnp.logical_not(last))
    def _():
        for i in range(pieces):
            y_keep(i).wait()

    for i in range(pieces):
        for side in range(2):
            r_copy(i, side).wait_recv()
    for copy in across:
        copy.wait_recv()

    def l_copy(k):
        return rdma(lo.at[k], lr.at[k], l_send.at[k], l_recv.at[k], level)

    def wgrad(b, k):
        left = sv[:, :, :, span(b * block, block)].reshape(NY * 4 * rows, block)
        right = gy[:, :, span(k * CW, CW)].reshape(NY * 4 * rows, CW)
        return tn_dot(left, right)

    def l_part(k, carry):
        lo[k] = wgrad(1 - l, k).astype(BF16)
        l_copy(k).start()
        return carry

    def l_own(k, carry):
        wg[:, span(k * CW, CW)] = wgrad(l, k)
        return carry

    def l_sum(k, carry):
        l_copy(k).wait_recv()
        wg[:, span(k * CW, CW)] = wg[:, span(k * CW, CW)] + lr[k].astype(F32)
        return carry

    parts = ((0, 128), (128, 256), (384, 256))

    def m_copy(k):
        here = pl.ds(*parts[k])
        return rdma(lo2.at[:, here], lr2.at[:, here], m_send.at[k], m_recv.at[k], level)

    def both(b, k):
        at, wide = parts[k]

        def part(ref, start):
            left = ref[:, :, :, span(b * block, block)].reshape(NY * 4 * rows, block)
            return tn_dot(left, gy[:, :, pl.ds(start + at, wide)].reshape(NY * 4 * rows, wide))

        return part(sv, 0) + part(sv2, block)

    def m_all():
        for k, (at, wide) in enumerate(parts):
            lo2[:, pl.ds(at, wide)] = both(1 - l, k).astype(BF16)
            m_copy(k).start()
        for k, (at, wide) in enumerate(parts):
            wg[:, span(l * block + at, wide)] = both(l, k)
        for k, (at, wide) in enumerate(parts):
            m_copy(k).wait_recv()
            wg[:, span((1 - l) * block + at, wide)] = lr2[:, pl.ds(at, wide)].astype(F32)

    @pl.when(last)
    def _():
        m_all()

    @pl.when(jnp.logical_not(last))
    def _():
        lax.fori_loop(0, nk, l_part, 0)
        lax.fori_loop(0, nk, l_own, 0)
        lax.fori_loop(0, nk, l_sum, 0)

    mine.wait()
    for copy in home:
        copy.wait_recv()
        copy.wait_send()
    for copy in across:
        copy.wait_send()
    for a in range(2):
        w_away[a].wait_send()
    for i in range(pieces):
        for side in range(2):
            r_copy(i, side).wait_send()

    @pl.when(last)
    def _():
        for i in range(pieces):
            g2_copy(i).wait_send()
            for side in range(2):
                y0_copy(i, side).wait_send()
                y2_copy(i, side).wait_send()
        for copy in lent + across2:
            copy.wait_send()
        for k in range(len(parts)):
            m_copy(k).wait_send()

    @pl.when(jnp.logical_not(last))
    def _():
        for i in range(pieces):
            for side in range(2):
                y_copy(i, side).wait_send()
        for k in range(nk):
            l_copy(k).wait_send()
    for chip in range(2):
        for dy in range(NY):
            for b in range(2):
                if chip or dy:
                    s_copy(chip, dy, b).wait_send()

    def drain(j, carry):
        p_copy(j).wait_send()

        @pl.when(s > 0)
        def _():
            x_copy(j).wait_send()

        @pl.when(jnp.logical_not(first))
        def _():
            f_copy(j).wait_send()

        return carry

    lax.fori_loop(0, total, drain, 0)


def put_out(own_input, weight_grad, inputs_out, weights_out, sems):
    copies = [
        pltpu.make_async_copy(own_input, inputs_out.at[0], sems.at[0]),
        pltpu.make_async_copy(weight_grad, weights_out.at[0], sems.at[1]),
    ]
    for copy in copies:
        copy.start()
    for copy in copies:
        copy.wait()


def on_device(saved, weight, out_grad):
    rows, width = out_grad.shape
    quarter, half = width // 4, width // 2
    nk = quarter // CW
    total = 4 * nk
    dma = pltpu.SemaphoreType.DMA
    vmem = pltpu.VMEM
    inside = pl.BlockSpec(memory_space=pltpu.VMEM)
    outside = pl.BlockSpec(memory_space=pltpu.HBM)
    anywhere = pl.BlockSpec(memory_space=pl.ANY)
    own_input, weight_grad = pl.pallas_call(
        relay,
        out_shape=(
            vmem((rows, width), BF16),
            vmem((quarter // 2, quarter), F32),
        ),
        in_specs=[outside, outside, outside],
        out_specs=(inside, inside),
        scratch_shapes=[
            vmem((2, quarter, half), BF16),
            vmem((4 * rows, half), BF16),
            vmem((total, rows, CW), BF16),
            vmem((total, rows, CW), BF16),
            vmem((total, rows, CW), F32),
            vmem((4 * rows, quarter), BF16),
            vmem((NY, 4 * rows, quarter), BF16),
            vmem((NY, 4, rows, quarter), BF16),
            vmem((nk, quarter // 2, CW), BF16),
            vmem((nk, quarter // 2, CW), BF16),
            vmem((NY, 4, rows, quarter), BF16),
            vmem((quarter // 2, quarter // 2), BF16),
            vmem((quarter // 2, quarter // 2), BF16),
            dma((2,)), dma((2,)), dma((2,)), dma((4,)), dma((4,)), dma((3,)), dma((3,)),
            dma((total,)), dma((total,)), dma((total,)), dma((total,)), dma((total,)), dma((total,)),
            dma((3,)), dma((3,)), dma((2, 4)), dma((2, 4)), dma((2, 4)), dma((2, 4)),
            dma((2, NY, 2)), dma((2, NY, 2)), dma((2,)), dma((2,)), dma((nk,)), dma((nk,)), dma((1,)), dma((4,)),
            dma((2, 4)), dma((2, 4)), dma((4,)), dma((4,)), dma((5,)), dma((5,)), dma((2,)), dma((2,)),
            dma((3,)), dma((3,)),
        ],
        compiler_params=pltpu.CompilerParams(
            collective_id=0, has_side_effects=True, vmem_limit_bytes=50 * 1024 * 1024
        ),
    )(out_grad, weight[0], saved[0])
    return pl.pallas_call(
        put_out,
        out_shape=(
            jax.ShapeDtypeStruct((1, rows, width), BF16),
            jax.ShapeDtypeStruct((1, quarter // 2, quarter), F32),
        ),
        in_specs=[inside, inside],
        out_specs=(outside, outside),
        scratch_shapes=[dma((2,))],
        compiler_params=pltpu.CompilerParams(vmem_limit_bytes=6 * 1024 * 1024),
    )(own_input, weight_grad)


def solution(mesh):
    placed = (
        P("section", ("dp", "tensor"), None),
        P("section", None, "tensor"),
        P(("dp", "tensor"), None),
    )
    return jax.shard_map(
        on_device,
        mesh=mesh,
        in_specs=placed,
        out_specs=(P("section", ("dp", "tensor"), None), P("section", "dp", "tensor")),
        check_vma=False,
    )
```

```python
import jax
import jax.numpy as jnp
from jax import lax
from jax.experimental import pallas as pl
from jax.experimental.pallas import tpu as pltpu
from jax.sharding import PartitionSpec as P

MESH = pl.DeviceIdType.MESH
BF16 = jnp.bfloat16
F32 = jnp.float32
CW = 256
NY = 4
SKEW = 7


def rdma(src, dst, send, recv, dev):
    return pltpu.make_async_remote_copy(
        src_ref=src, dst_ref=dst, send_sem=send, recv_sem=recv, device_id=dev, device_id_type=MESH
    )


def nt_dot(a, b):
    return lax.dot_general(a, b, (((1,), (1,)), ((), ())), preferred_element_type=F32)


def tn_dot(a, b):
    return lax.dot_general(a, b, (((0,), (0,)), ((), ())), preferred_element_type=F32)


def span(start, size):
    return pl.ds(pl.multiple_of(start, 128), size)


def relay(
    og, w, saved,
    out, wg,
    wv, g, ps, pr, own, gn, gy, sv, lo, lr, sv2, lo2, lr2,
    w_sem, w_send, w_recv, gi_send, gi_recv, gf_send, gf_recv, x_send, x_recv, f_send, f_recv, p_send, p_recv,
    o_send, o_recv, y_send, y_recv, r_send, r_recv, s_send, s_recv, t_send, t_recv, l_send, l_recv, loc, yloc,
    y2_send, y2_recv, g2_send, g2_recv, u_send, u_recv, v_send, v_recv, m_send, m_recv,
):
    rows, width = og.shape
    quarter, half = width // 4, width // 2
    nk = quarter // CW
    pieces = 4
    total = pieces * nk
    block = quarter // 2
    sections = lax.axis_size("section")
    s, d, t = lax.axis_index("section"), lax.axis_index("dp"), lax.axis_index("tensor")
    l, y = d // NY, d % NY
    h, c = t // 2, t % 2
    partner_t = h * 2 + 1 - c
    pair_t = (1 - h) * 2 + c
    cross_t = (1 - h) * 2 + 1 - c
    pair_l = (1 - l) * NY
    partner = (s, d, partner_t)
    pair = (s, pair_l + y, pair_t)
    cross = (s, pair_l + y, cross_t)
    level = (s, pair_l + y, t)
    up = (lax.rem(s + sections - 1, sections), d, t)
    down = (lax.rem(s + 1, sections), d, t)
    first = s == sections - 1
    ys = [lax.rem(y + dy, NY) for dy in range(NY)]
    along = [(s, l * NY + ys[dy], t) for dy in range(NY)]
    pair_along = [(s, pair_l + ys[dy], pair_t) for dy in range(NY)]

    barrier = pltpu.get_barrier_semaphore()
    friends = [partner, pair, cross, level, up, down] + along[1:] + pair_along[1:]
    for dev in friends:
        pl.semaphore_signal(barrier, inc=1, device_id=dev, device_id_type=MESH)
    pl.semaphore_wait(barrier, len(friends))

    cols = span(c * quarter, quarter)
    t_cols = span(t * quarter, quarter)
    own_rows = span(t * rows, rows)
    pair_rows = span(pair_t * rows, rows)
    my_half = span(h * half, half)
    other_half = span((1 - h) * half, half)

    cuts = (0, half * 7 // 20, half * 14 // 20, half)

    def g_there(q):
        return pl.ds(cuts[q], cuts[q + 1] - cuts[q])

    def g_cols(q):
        return span((1 - h) * half + cuts[q], cuts[q + 1] - cuts[q])

    def g_fwd(q):
        here = g.at[pair_rows, g_there(q)]
        return rdma(here, here, gf_send.at[q], gf_recv.at[q], partner)

    g_pair = rdma(og.at[:, g_cols(0)], g.at[own_rows, g_there(0)], gi_send.at[0], gi_recv.at[0], pair)

    def g_lend(q):
        there = gn.at[pl.ds(0, rows), pl.ds(0, cuts[q + 1] - cuts[q])]
        return rdma(og.at[:, g_cols(q)], there, gf_send.at[q], gf_recv.at[q], pair)

    def g_relay(q, dev):
        here = gn.at[pl.ds(0, rows), pl.ds(0, cuts[q + 1] - cuts[q])]
        return rdma(here, g.at[pair_rows, g_there(q)], gi_send.at[q], gi_recv.at[q], dev)

    beside = [(1, s == sections - 2, down), (2, s == 0, up)]

    @pl.when(first)
    def _():
        g_pair.start()

    for q, lends, dev in beside:
        @pl.when(lends)
        def _():
            g_lend(q).start()

    g_partner = rdma(og.at[:, my_half], g.at[own_rows, :], gi_send.at[3], gi_recv.at[3], partner)

    @pl.when(first)
    def _():
        g_partner.start()

    def w_rows(a, core):
        hh = (1 - h) if a == 0 else h
        return span(hh * half + core * quarter, quarter)

    w_local = [pltpu.make_async_copy(w.at[w_rows(a, c), :], wv.at[a, :, cols], w_sem.at[a]) for a in range(2)]
    w_away = [rdma(w.at[w_rows(a, 1 - c), :], wv.at[a, :, cols], w_send.at[a], w_recv.at[a], partner) for a in range(2)]
    w_away[0].start()
    w_local[0].start()
    w_local[1].start()

    @pl.when(jnp.logical_not(first))
    def _():
        w_away[1].start()

    for q, lends, dev in beside:
        @pl.when(lends)
        def _():
            g_lend(q).wait_recv()
            g_relay(q, dev).start()

    def s_copy(chip, dy, b):
        src = saved.at[:, span(b * half + ys[dy] * block, block)]
        dst = sv.at[y, t, :, pl.ds(b * block, block)]
        if chip == 0 and dy == 0:
            return pltpu.make_async_copy(src, dst, s_recv.at[0, y, b])
        dev = along[dy] if chip == 0 else pair_along[dy]
        return rdma(src, dst, s_send.at[chip, dy, b], s_recv.at[chip, y, b], dev)

    def s_start(chip, dys):
        for dy in dys:
            for b in range(2):
                s_copy(chip, dy, b).start()

    s_start(0, range(NY))

    @pl.when(s < sections - 1)
    def _():
        s_start(1, (1, 2))

    @pl.when(s < sections - 2)
    def _():
        s_start(1, (0, 3))

    def piece_rows(i):
        return span(i * rows, rows)

    def at(j):
        i, k = j // nk, j % nk
        return piece_rows(i), k * CW

    def x_copy(j):
        r, k = at(j)
        return rdma(gn.at[r, span(k, CW)], g.at[r, span(c * quarter + k, CW)], x_send.at[j], x_recv.at[j], up)

    def f_copy(j):
        r, k = at(j)
        here = g.at[r, span(c * quarter + k, CW)]
        return rdma(here, here, f_send.at[j], f_recv.at[j], partner)

    def p_copy(j):
        return rdma(ps.at[j], pr.at[j], p_send.at[j], p_recv.at[j], pair)

    def y_copy(i, side):
        r = piece_rows(i)
        dev = along[1] if side == 0 else along[NY - 1]
        return rdma(g.at[r, cols], gy.at[y, r, :], y_send.at[side, i], y_recv.at[side, i], dev)

    def y_keep(i):
        r = piece_rows(i)
        return pltpu.make_async_copy(g.at[r, cols], gy.at[y, r, :], yloc.at[i])

    def r_copy(i, side):
        here = gy.at[ys[NY - 1] if side == 0 else ys[1], piece_rows(i), pl.ds(side * block, block)]
        dev = along[1] if side == 0 else along[NY - 1]
        return rdma(here, here, r_send.at[side, i], r_recv.at[side, i], dev)

    last = s == 0
    l_half = span(c * quarter + l * block, block)
    near, far = pl.ds(0, block), pl.ds(block, block)

    def g2_copy(i):
        r = piece_rows(i)
        return rdma(
            g.at[r, span(c * quarter + (1 - l) * block, block)], gy.at[y, r, far], g2_send.at[i], g2_recv.at[i], level
        )

    def y0_copy(i, side):
        r = piece_rows(i)
        dev = along[1] if side == 0 else along[NY - 1]
        return rdma(g.at[r, l_half], gy.at[y, r, near], y_send.at[side, i], y_recv.at[side, i], dev)

    def y2_copy(i, side):
        here = gy.at[y, piece_rows(i), far]
        dev = along[1] if side == 0 else along[NY - 1]
        return rdma(here, here, y2_send.at[side, i], y2_recv.at[side, i], dev)

    def y0_keep(i):
        r = piece_rows(i)
        return pltpu.make_async_copy(g.at[r, l_half], gy.at[y, r, near], yloc.at[i])

    def spread(i):
        @pl.when(last)
        def _():
            g2_copy(i).start()
            for side in range(2):
                y0_copy(i, side).start()
            y0_keep(i).start()

        @pl.when(jnp.logical_not(last))
        def _():
            for side in range(2):
                y_copy(i, side).start()
            y_keep(i).start()

    def spread_far(i):
        g2_copy(i).wait_recv()
        for side in range(2):
            y2_copy(i, side).start()

    def pass_near(i):
        y0_copy(i, 0).wait_recv()
        r_copy(i, 0).start()

    def pass_far(i):
        y2_copy(i, 1).wait_recv()
        r_copy(i, 1).start()

    def pass_on(i):
        for side in range(2):
            y_copy(i, side).wait_recv()
            r_copy(i, side).start()

    @pl.when(first)
    def _():
        here = pltpu.make_async_copy(og.at[:, my_half], g.at[own_rows, :], loc.at[0])
        here.start()
        g_pair.wait_recv()
        g_fwd(0).start()
        for q, lends, dev in beside:
            g_relay(q, dev).wait_recv()
            g_fwd(q).start()
        w_away[1].start()
        here.wait()
        g_partner.wait_recv()
        g_partner.wait_send()
        g_pair.wait_send()
        for q in range(3):
            g_fwd(q).wait_recv()
            g_fwd(q).wait_send()

    for q, lends, dev in beside:
        @pl.when(lends)
        def _():
            g_lend(q).wait_send()
            g_relay(q, dev).wait_send()

    tokens = [sv.at[:, c], sv.at[:, 2 + c]]
    across = [rdma(ref, ref, t_send.at[i], t_recv.at[i], partner) for i, ref in enumerate(tokens)]

    def s_arrived(chip):
        for yy in range(NY):
            for b in range(2):
                where = sv.at[yy, 0, :, pl.ds(b * block, block)]
                pltpu.make_async_copy(where, where, s_recv.at[chip, yy, b]).wait()

    def s_across():
        for copy in across:
            copy.start()

    beyond = [(sv.at[:, t], sv2.at[:, t]), (sv.at[:, pair_t], sv2.at[:, pair_t])]
    lent = [rdma(*beyond[0], u_send.at[0], u_recv.at[0], level)] + [
        rdma(sv.at[yy, pair_t], sv2.at[yy, pair_t], u_send.at[1 + yy], u_recv.at[1 + yy], level) for yy in range(NY)
    ]
    across2 = [rdma(dst, dst, v_send.at[i], v_recv.at[i], partner) for i, (src, dst) in enumerate(beyond)]

    @pl.when(last)
    def _():
        s_arrived(0)
        lent[0].start()
        s_arrived(1)
        lent[1].start()
        lent[2].start()
        s_across()

    def step(j, carry):
        i, k = j // nk, j % nk

        @pl.when(jnp.logical_and(j < total, jnp.logical_not(first)))
        def _():
            x_copy(j).wait_recv()
            f_copy(j).start()

        @pl.when(j >= SKEW)
        def _():
            f = j - SKEW
            r, kk = at(f)
            p_copy(f).wait_recv()
            summed = own[f] + pr[f].astype(F32) + g[r, span(c * quarter + kk, CW)].astype(F32)
            gn[r, span(kk, CW)] = summed.astype(BF16)

            @pl.when(s > 0)
            def _():
                x_copy(f).start()

        @pl.when(jnp.logical_and(j < total, k == nk - 1))
        def _():
            spread(i)
            for q in range(2):
                @pl.when(jnp.logical_and(last, i == q))
                def _():
                    lent[3 + q].start()

            @pl.when(jnp.logical_and(last, i > 0))
            def _():
                pass_near(i - 1)

            @pl.when(jnp.logical_not(first))
            def _():
                def forwarded(q, carry):
                    f_copy(i * nk + q).wait_recv()
                    return carry

                lax.fori_loop(0, nk, forwarded, 0)

            @pl.when(i == 0)
            def _():
                w_local[0].wait()
                w_away[0].wait_recv()

            def send_part(q, carry):
                f = i * nk + q
                ps[f] = nt_dot(g[piece_rows(i), :], wv[0, span(q * CW, CW), :]).astype(BF16)
                p_copy(f).start()
                return carry

            lax.fori_loop(0, nk, send_part, 0)

            @pl.when(i == 0)
            def _():
                w_local[1].wait()
                w_away[1].wait_recv()

            @pl.when(jnp.logical_and(last, i == 3))
            def _():
                for copy in lent:
                    copy.wait_recv()
                for on in across2:
                    on.start()

            @pl.when(jnp.logical_and(jnp.logical_not(last), i >= 2))
            def _():
                pass_on(i - 2)

        @pl.when(jnp.logical_and(last, jnp.logical_and(j < total, k == nk - 2)))
        def _():
            @pl.when(i >= 1)
            def _():
                spread_far(i - 1)

            @pl.when(i >= 2)
            def _():
                pass_far(i - 2)

        @pl.when(j == total)
        def _():
            @pl.when(last)
            def _():
                spread_far(pieces - 1)
                pass_far(pieces - 2)
                pass_near(pieces - 1)

            @pl.when(jnp.logical_not(last))
            def _():
                pass_on(pieces - 2)

        @pl.when(j == total + 4)
        def _():
            @pl.when(last)
            def _():
                pass_far(pieces - 1)

            @pl.when(jnp.logical_not(last))
            def _():
                pass_on(pieces - 1)

        @pl.when(jnp.logical_and(j >= nk, j < total + nk))
        def _():
            f = j - nk
            r, kk = at(f)
            own[f] = nt_dot(g[r, :], wv[1, span(kk, CW), :])

        return carry

    lax.fori_loop(0, total + SKEW, step, 0)

    @pl.when(s == sections - 1)
    def _():
        s_start(1, (1, 2))

    @pl.when(s >= sections - 2)
    def _():
        s_start(1, (0, 3))

    homes = [partner, pair, cross]
    blocks = [partner_t, pair_t, cross_t]
    home = [
        rdma(gn.at[span(b * rows, rows), :], out.at[:, t_cols], o_send.at[i], o_recv.at[i], dev)
        for i, (dev, b) in enumerate(zip(homes, blocks))
    ]
    for copy in home:
        copy.start()
    mine = pltpu.make_async_copy(gn.at[own_rows, :], out.at[:, t_cols], loc.at[0])
    mine.start()


    @pl.when(s > 0)
    def _():
        for chip in range(2):
            s_arrived(chip)
        s_across()

    for copy in across:
        copy.wait_recv()

    @pl.when(last)
    def _():
        for i in range(pieces):
            y0_keep(i).wait()
            y0_copy(i, 1).wait_recv()
            r_copy(i, 0).wait_recv()

    @pl.when(jnp.logical_not(last))
    def _():
        for i in range(pieces):
            y_keep(i).wait()
            for side in range(2):
                r_copy(i, side).wait_recv()

    def l_copy(k):
        return rdma(lo.at[k], lr.at[k], l_send.at[k], l_recv.at[k], level)

    def wgrad(b, k):
        left = sv[:, :, :, span(b * block, block)].reshape(NY * 4 * rows, block)
        right = gy[:, :, span(k * CW, CW)].reshape(NY * 4 * rows, CW)
        return tn_dot(left, right)

    def l_part(k, carry):
        lo[k] = wgrad(1 - l, k).astype(BF16)
        l_copy(k).start()
        return carry

    def l_own(k, carry):
        wg[:, span(k * CW, CW)] = wgrad(l, k)
        return carry

    def l_sum(k, carry):
        l_copy(k).wait_recv()
        wg[:, span(k * CW, CW)] = wg[:, span(k * CW, CW)] + lr[k].astype(F32)
        return carry

    parts = ((0, 128), (128, 256), (384, 256))

    def m_copy(k):
        here = pl.ds(*parts[k])
        return rdma(lo2.at[:, here], lr2.at[:, here], m_send.at[k], m_recv.at[k], level)

    def part(ref, start, b, k):
        at, wide = parts[k]
        left = ref[:, :, :, span(b * block, block)].reshape(NY * 4 * rows, block)
        return tn_dot(left, gy[:, :, pl.ds(start + at, wide)].reshape(NY * 4 * rows, wide))

    def both(b, k):
        return part(sv, 0, b, k) + part(sv2, block, b, k)

    def m_all():
        for k, (at, wide) in enumerate(parts):
            wg[:, span((1 - l) * block + at, wide)] = part(sv, 0, 1 - l, k)
        for on in across2:
            on.wait_recv()
        for i in range(pieces):
            y2_copy(i, 0).wait_recv()
            r_copy(i, 1).wait_recv()
        for k, (at, wide) in enumerate(parts):
            near_sum = wg[:, span((1 - l) * block + at, wide)]
            lo2[:, pl.ds(at, wide)] = (near_sum + part(sv2, block, 1 - l, k)).astype(BF16)
            m_copy(k).start()
        for k, (at, wide) in enumerate(parts):
            wg[:, span(l * block + at, wide)] = both(l, k)
        for k, (at, wide) in enumerate(parts):
            m_copy(k).wait_recv()
            wg[:, span((1 - l) * block + at, wide)] = lr2[:, pl.ds(at, wide)].astype(F32)

    @pl.when(last)
    def _():
        m_all()

    @pl.when(jnp.logical_not(last))
    def _():
        lax.fori_loop(0, nk, l_part, 0)
        lax.fori_loop(0, nk, l_own, 0)
        lax.fori_loop(0, nk, l_sum, 0)

    mine.wait()
    for copy in home:
        copy.wait_recv()
        copy.wait_send()
    for copy in across:
        copy.wait_send()
    for a in range(2):
        w_away[a].wait_send()
    for i in range(pieces):
        for side in range(2):
            r_copy(i, side).wait_send()

    @pl.when(last)
    def _():
        for i in range(pieces):
            g2_copy(i).wait_send()
            for side in range(2):
                y0_copy(i, side).wait_send()
                y2_copy(i, side).wait_send()
        for copy in lent + across2:
            copy.wait_send()
        for k in range(len(parts)):
            m_copy(k).wait_send()

    @pl.when(jnp.logical_not(last))
    def _():
        for i in range(pieces):
            for side in range(2):
                y_copy(i, side).wait_send()
        for k in range(nk):
            l_copy(k).wait_send()
    for chip in range(2):
        for dy in range(NY):
            for b in range(2):
                if chip or dy:
                    s_copy(chip, dy, b).wait_send()

    def drain(j, carry):
        p_copy(j).wait_send()

        @pl.when(s > 0)
        def _():
            x_copy(j).wait_send()

        @pl.when(jnp.logical_not(first))
        def _():
            f_copy(j).wait_send()

        return carry

    lax.fori_loop(0, total, drain, 0)


def put_out(own_input, weight_grad, inputs_out, weights_out, sems):
    copies = [
        pltpu.make_async_copy(own_input, inputs_out.at[0], sems.at[0]),
        pltpu.make_async_copy(weight_grad, weights_out.at[0], sems.at[1]),
    ]
    for copy in copies:
        copy.start()
    for copy in copies:
        copy.wait()


def on_device(saved, weight, out_grad):
    rows, width = out_grad.shape
    quarter, half = width // 4, width // 2
    nk = quarter // CW
    total = 4 * nk
    dma = pltpu.SemaphoreType.DMA
    vmem = pltpu.VMEM
    inside = pl.BlockSpec(memory_space=pltpu.VMEM)
    outside = pl.BlockSpec(memory_space=pltpu.HBM)
    anywhere = pl.BlockSpec(memory_space=pl.ANY)
    own_input, weight_grad = pl.pallas_call(
        relay,
        out_shape=(
            vmem((rows, width), BF16),
            vmem((quarter // 2, quarter), F32),
        ),
        in_specs=[outside, outside, outside],
        out_specs=(inside, inside),
        scratch_shapes=[
            vmem((2, quarter, half), BF16),
            vmem((4 * rows, half), BF16),
            vmem((total, rows, CW), BF16),
            vmem((total, rows, CW), BF16),
            vmem((total, rows, CW), F32),
            vmem((4 * rows, quarter), BF16),
            vmem((NY, 4 * rows, quarter), BF16),
            vmem((NY, 4, rows, quarter), BF16),
            vmem((nk, quarter // 2, CW), BF16),
            vmem((nk, quarter // 2, CW), BF16),
            vmem((NY, 4, rows, quarter), BF16),
            vmem((quarter // 2, quarter // 2), BF16),
            vmem((quarter // 2, quarter // 2), BF16),
            dma((2,)), dma((2,)), dma((2,)), dma((4,)), dma((4,)), dma((3,)), dma((3,)),
            dma((total,)), dma((total,)), dma((total,)), dma((total,)), dma((total,)), dma((total,)),
            dma((3,)), dma((3,)), dma((2, 4)), dma((2, 4)), dma((2, 4)), dma((2, 4)),
            dma((2, NY, 2)), dma((2, NY, 2)), dma((2,)), dma((2,)), dma((nk,)), dma((nk,)), dma((1,)), dma((4,)),
            dma((2, 4)), dma((2, 4)), dma((4,)), dma((4,)), dma((5,)), dma((5,)), dma((2,)), dma((2,)),
            dma((3,)), dma((3,)),
        ],
        compiler_params=pltpu.CompilerParams(
            collective_id=0, has_side_effects=True, vmem_limit_bytes=50 * 1024 * 1024
        ),
    )(out_grad, weight[0], saved[0])
    return pl.pallas_call(
        put_out,
        out_shape=(
            jax.ShapeDtypeStruct((1, rows, width), BF16),
            jax.ShapeDtypeStruct((1, quarter // 2, quarter), F32),
        ),
        in_specs=[inside, inside],
        out_specs=(outside, outside),
        scratch_shapes=[dma((2,))],
        compiler_params=pltpu.CompilerParams(vmem_limit_bytes=6 * 1024 * 1024),
    )(own_input, weight_grad)


def solution(mesh):
    placed = (
        P("section", ("dp", "tensor"), None),
        P("section", None, "tensor"),
        P(("dp", "tensor"), None),
    )
    return jax.shard_map(
        on_device,
        mesh=mesh,
        in_specs=placed,
        out_specs=(P("section", ("dp", "tensor"), None), P("section", "dp", "tensor")),
        check_vma=False,
    )
```

```python
import jax
import jax.numpy as jnp
from jax import lax
from jax.experimental import pallas as pl
from jax.experimental.pallas import tpu as pltpu
from jax.sharding import PartitionSpec as P

MESH = pl.DeviceIdType.MESH
BF16 = jnp.bfloat16
F32 = jnp.float32
CW = 256
NY = 4
SKEW = 7


def rdma(src, dst, send, recv, dev):
    return pltpu.make_async_remote_copy(
        src_ref=src, dst_ref=dst, send_sem=send, recv_sem=recv, device_id=dev, device_id_type=MESH
    )


def nt_dot(a, b):
    return lax.dot_general(a, b, (((1,), (1,)), ((), ())), preferred_element_type=F32)


def tn_dot(a, b):
    return lax.dot_general(a, b, (((0,), (0,)), ((), ())), preferred_element_type=F32)


def span(start, size):
    return pl.ds(pl.multiple_of(start, 128), size)


def relay(
    og, w, saved,
    out, wg,
    wv, g, ps, pr, own, gn, gy, sv, lo, lr, sv2, lo2, lr2,
    w_sem, w_send, w_recv, gi_send, gi_recv, gf_send, gf_recv, x_send, x_recv, f_send, f_recv, p_send, p_recv,
    o_send, o_recv, y_send, y_recv, r_send, r_recv, s_send, s_recv, t_send, t_recv, l_send, l_recv, loc, yloc,
    y2_send, y2_recv, g2_send, g2_recv, u_send, u_recv, v_send, v_recv, m_send, m_recv,
):
    rows, width = og.shape
    quarter, half = width // 4, width // 2
    nk = quarter // CW
    pieces = 4
    total = pieces * nk
    block = quarter // 2
    sections = lax.axis_size("section")
    s, d, t = lax.axis_index("section"), lax.axis_index("dp"), lax.axis_index("tensor")
    l, y = d // NY, d % NY
    h, c = t // 2, t % 2
    partner_t = h * 2 + 1 - c
    pair_t = (1 - h) * 2 + c
    cross_t = (1 - h) * 2 + 1 - c
    pair_l = (1 - l) * NY
    partner = (s, d, partner_t)
    pair = (s, pair_l + y, pair_t)
    cross = (s, pair_l + y, cross_t)
    level = (s, pair_l + y, t)
    up = (lax.rem(s + sections - 1, sections), d, t)
    down = (lax.rem(s + 1, sections), d, t)
    first = s == sections - 1
    ys = [lax.rem(y + dy, NY) for dy in range(NY)]
    along = [(s, l * NY + ys[dy], t) for dy in range(NY)]
    pair_along = [(s, pair_l + ys[dy], pair_t) for dy in range(NY)]

    barrier = pltpu.get_barrier_semaphore()
    friends = [partner, pair, cross, level, up, down] + along[1:] + pair_along[1:]
    for dev in friends:
        pl.semaphore_signal(barrier, inc=1, device_id=dev, device_id_type=MESH)
    pl.semaphore_wait(barrier, len(friends))

    cols = span(c * quarter, quarter)
    t_cols = span(t * quarter, quarter)
    own_rows = span(t * rows, rows)
    pair_rows = span(pair_t * rows, rows)
    my_half = span(h * half, half)
    other_half = span((1 - h) * half, half)

    cuts = (0, half * 7 // 20, half * 14 // 20, half)

    def g_there(q):
        return pl.ds(cuts[q], cuts[q + 1] - cuts[q])

    def g_cols(q):
        return span((1 - h) * half + cuts[q], cuts[q + 1] - cuts[q])

    def g_fwd(q):
        here = g.at[pair_rows, g_there(q)]
        return rdma(here, here, gf_send.at[q], gf_recv.at[q], partner)

    g_pair = rdma(og.at[:, g_cols(0)], g.at[own_rows, g_there(0)], gi_send.at[0], gi_recv.at[0], pair)

    def g_lend(q):
        there = gn.at[pl.ds(0, rows), pl.ds(0, cuts[q + 1] - cuts[q])]
        return rdma(og.at[:, g_cols(q)], there, gf_send.at[q], gf_recv.at[q], pair)

    def g_relay(q, dev):
        here = gn.at[pl.ds(0, rows), pl.ds(0, cuts[q + 1] - cuts[q])]
        return rdma(here, g.at[pair_rows, g_there(q)], gi_send.at[q], gi_recv.at[q], dev)

    beside = [(1, s == sections - 2, down), (2, s == 0, up)]

    @pl.when(first)
    def _():
        g_pair.start()

    for q, lends, dev in beside:
        @pl.when(lends)
        def _():
            g_lend(q).start()

    g_partner = rdma(og.at[:, my_half], g.at[own_rows, :], gi_send.at[3], gi_recv.at[3], partner)

    @pl.when(first)
    def _():
        g_partner.start()

    def w_rows(a, core):
        hh = (1 - h) if a == 0 else h
        return span(hh * half + core * quarter, quarter)

    w_local = [pltpu.make_async_copy(w.at[w_rows(a, c), :], wv.at[a, :, cols], w_sem.at[a]) for a in range(2)]
    w_away = [rdma(w.at[w_rows(a, 1 - c), :], wv.at[a, :, cols], w_send.at[a], w_recv.at[a], partner) for a in range(2)]
    w_away[0].start()
    w_local[0].start()
    w_local[1].start()

    @pl.when(jnp.logical_not(first))
    def _():
        w_away[1].start()

    for q, lends, dev in beside:
        @pl.when(lends)
        def _():
            g_lend(q).wait_recv()
            g_relay(q, dev).start()

    def s_copy(chip, dy, b):
        src = saved.at[:, span(b * half + ys[dy] * block, block)]
        dst = sv.at[y, t, :, pl.ds(b * block, block)]
        if chip == 0 and dy == 0:
            return pltpu.make_async_copy(src, dst, s_recv.at[0, y, b])
        dev = along[dy] if chip == 0 else pair_along[dy]
        return rdma(src, dst, s_send.at[chip, dy, b], s_recv.at[chip, y, b], dev)

    def s_start(chip, dys):
        for dy in dys:
            for b in range(2):
                s_copy(chip, dy, b).start()

    s_start(0, range(NY))

    @pl.when(s < sections - 1)
    def _():
        s_start(1, (1, 2))

    @pl.when(s < sections - 2)
    def _():
        s_start(1, (0, 3))

    def piece_rows(i):
        return span(i * rows, rows)

    def at(j):
        i, k = j // nk, j % nk
        return piece_rows(i), k * CW

    def x_copy(j):
        r, k = at(j)
        return rdma(gn.at[r, span(k, CW)], g.at[r, span(c * quarter + k, CW)], x_send.at[j], x_recv.at[j], up)

    def f_copy(j):
        r, k = at(j)
        here = g.at[r, span(c * quarter + k, CW)]
        return rdma(here, here, f_send.at[j], f_recv.at[j], partner)

    def p_copy(j):
        return rdma(ps.at[j], pr.at[j], p_send.at[j], p_recv.at[j], pair)

    def y_copy(i, side):
        r = piece_rows(i)
        dev = along[1] if side == 0 else along[NY - 1]
        return rdma(g.at[r, cols], gy.at[y, r, :], y_send.at[side, i], y_recv.at[side, i], dev)

    def y_keep(i):
        r = piece_rows(i)
        return pltpu.make_async_copy(g.at[r, cols], gy.at[y, r, :], yloc.at[i])

    def r_copy(i, side):
        here = gy.at[ys[NY - 1] if side == 0 else ys[1], piece_rows(i), pl.ds(side * block, block)]
        dev = along[1] if side == 0 else along[NY - 1]
        return rdma(here, here, r_send.at[side, i], r_recv.at[side, i], dev)

    last = s == 0
    l_half = span(c * quarter + l * block, block)
    near, far = pl.ds(0, block), pl.ds(block, block)

    def g2_copy(i):
        r = piece_rows(i)
        return rdma(
            g.at[r, span(c * quarter + (1 - l) * block, block)], gy.at[y, r, far], g2_send.at[i], g2_recv.at[i], level
        )

    def y0_copy(i, side):
        r = piece_rows(i)
        dev = along[1] if side == 0 else along[NY - 1]
        return rdma(g.at[r, l_half], gy.at[y, r, near], y_send.at[side, i], y_recv.at[side, i], dev)

    def y2_copy(i, side):
        here = gy.at[y, piece_rows(i), far]
        dev = along[1] if side == 0 else along[NY - 1]
        return rdma(here, here, y2_send.at[side, i], y2_recv.at[side, i], dev)

    def y0_keep(i):
        r = piece_rows(i)
        return pltpu.make_async_copy(g.at[r, l_half], gy.at[y, r, near], yloc.at[i])

    def spread(i):
        @pl.when(last)
        def _():
            g2_copy(i).start()
            for side in range(2):
                y0_copy(i, side).start()
            y0_keep(i).start()

        @pl.when(jnp.logical_not(last))
        def _():
            for side in range(2):
                y_copy(i, side).start()
            y_keep(i).start()

    def spread_far(i):
        g2_copy(i).wait_recv()
        for side in range(2):
            y2_copy(i, side).start()

    def pass_near(i):
        y0_copy(i, 0).wait_recv()
        r_copy(i, 0).start()

    def pass_far(i):
        y2_copy(i, 1).wait_recv()
        r_copy(i, 1).start()

    def pass_on(i):
        for side in range(2):
            y_copy(i, side).wait_recv()
            r_copy(i, side).start()

    @pl.when(first)
    def _():
        here = pltpu.make_async_copy(og.at[:, my_half], g.at[own_rows, :], loc.at[0])
        here.start()
        g_pair.wait_recv()
        g_fwd(0).start()
        for q, lends, dev in beside:
            g_relay(q, dev).wait_recv()
            g_fwd(q).start()
        w_away[1].start()
        here.wait()
        g_partner.wait_recv()
        g_partner.wait_send()
        g_pair.wait_send()
        for q in range(3):
            g_fwd(q).wait_recv()
            g_fwd(q).wait_send()

    for q, lends, dev in beside:
        @pl.when(lends)
        def _():
            g_lend(q).wait_send()
            g_relay(q, dev).wait_send()

    tokens = [sv.at[:, c], sv.at[:, 2 + c]]
    across = [rdma(ref, ref, t_send.at[i], t_recv.at[i], partner) for i, ref in enumerate(tokens)]

    def s_arrived(chip):
        for yy in range(NY):
            for b in range(2):
                where = sv.at[yy, 0, :, pl.ds(b * block, block)]
                pltpu.make_async_copy(where, where, s_recv.at[chip, yy, b]).wait()

    def s_across():
        for copy in across:
            copy.start()

    beyond = [(sv.at[:, t], sv2.at[:, t]), (sv.at[:, pair_t], sv2.at[:, pair_t])]
    lent = [rdma(*beyond[0], u_send.at[0], u_recv.at[0], level)] + [
        rdma(sv.at[yy, pair_t], sv2.at[yy, pair_t], u_send.at[1 + yy], u_recv.at[1 + yy], level) for yy in range(NY)
    ]
    across2 = [rdma(dst, dst, v_send.at[i], v_recv.at[i], partner) for i, (src, dst) in enumerate(beyond)]

    @pl.when(last)
    def _():
        s_arrived(0)
        lent[0].start()
        s_arrived(1)
        lent[1].start()
        lent[2].start()
        s_across()

    def step(j, carry):
        i, k = j // nk, j % nk

        @pl.when(jnp.logical_and(j < total, jnp.logical_not(first)))
        def _():
            x_copy(j).wait_recv()
            f_copy(j).start()

        @pl.when(j >= SKEW)
        def _():
            f = j - SKEW
            r, kk = at(f)
            p_copy(f).wait_recv()
            summed = own[f] + pr[f].astype(F32) + g[r, span(c * quarter + kk, CW)].astype(F32)
            gn[r, span(kk, CW)] = summed.astype(BF16)

            @pl.when(s > 0)
            def _():
                x_copy(f).start()

        @pl.when(jnp.logical_and(j < total, k == nk - 1))
        def _():
            spread(i)
            for q in range(2):
                @pl.when(jnp.logical_and(last, i == q))
                def _():
                    lent[3 + q].start()

            @pl.when(jnp.logical_and(last, i > 0))
            def _():
                pass_near(i - 1)

            @pl.when(jnp.logical_not(first))
            def _():
                def forwarded(q, carry):
                    f_copy(i * nk + q).wait_recv()
                    return carry

                lax.fori_loop(0, nk, forwarded, 0)

            @pl.when(i == 0)
            def _():
                w_local[0].wait()
                w_away[0].wait_recv()

            def send_part(q, carry):
                f = i * nk + q
                ps[f] = nt_dot(g[piece_rows(i), :], wv[0, span(q * CW, CW), :]).astype(BF16)
                p_copy(f).start()
                return carry

            lax.fori_loop(0, nk, send_part, 0)

            @pl.when(i == 0)
            def _():
                w_local[1].wait()
                w_away[1].wait_recv()

            @pl.when(jnp.logical_and(last, i == 3))
            def _():
                for copy in lent:
                    copy.wait_recv()
                for on in across2:
                    on.start()

            @pl.when(jnp.logical_and(jnp.logical_not(last), i >= 2))
            def _():
                pass_on(i - 2)

        @pl.when(jnp.logical_and(last, jnp.logical_and(j < total, k == nk - 2)))
        def _():
            @pl.when(i >= 1)
            def _():
                spread_far(i - 1)

            @pl.when(i >= 2)
            def _():
                pass_far(i - 2)

        @pl.when(j == total)
        def _():
            @pl.when(last)
            def _():
                spread_far(pieces - 1)
                pass_far(pieces - 2)
                pass_near(pieces - 1)

            @pl.when(jnp.logical_not(last))
            def _():
                pass_on(pieces - 2)

        @pl.when(j == total + 4)
        def _():
            @pl.when(last)
            def _():
                pass_far(pieces - 1)

            @pl.when(jnp.logical_not(last))
            def _():
                pass_on(pieces - 1)

        @pl.when(jnp.logical_and(j >= nk, j < total + nk))
        def _():
            f = j - nk
            r, kk = at(f)
            own[f] = nt_dot(g[r, :], wv[1, span(kk, CW), :])

        return carry

    lax.fori_loop(0, total + SKEW, step, 0)

    @pl.when(s == sections - 1)
    def _():
        s_start(1, (1, 2))

    @pl.when(s >= sections - 2)
    def _():
        s_start(1, (0, 3))

    homes = [partner, pair, cross]
    blocks = [partner_t, pair_t, cross_t]
    home = [
        rdma(gn.at[span(b * rows, rows), :], out.at[:, t_cols], o_send.at[i], o_recv.at[i], dev)
        for i, (dev, b) in enumerate(zip(homes, blocks))
    ]
    for copy in home:
        copy.start()
    mine = pltpu.make_async_copy(gn.at[own_rows, :], out.at[:, t_cols], loc.at[0])
    mine.start()


    @pl.when(s > 0)
    def _():
        for chip in range(2):
            s_arrived(chip)
        s_across()

    for copy in across:
        copy.wait_recv()

    @pl.when(last)
    def _():
        for i in range(pieces):
            y0_keep(i).wait()
            y0_copy(i, 1).wait_recv()
            r_copy(i, 0).wait_recv()

    @pl.when(jnp.logical_not(last))
    def _():
        for i in range(pieces):
            y_keep(i).wait()
            for side in range(2):
                r_copy(i, side).wait_recv()

    def l_copy(k):
        return rdma(lo.at[k], lr.at[k], l_send.at[k], l_recv.at[k], level)

    def wgrad(b, k):
        left = sv[:, :, :, span(b * block, block)].reshape(NY * 4 * rows, block)
        right = gy[:, :, span(k * CW, CW)].reshape(NY * 4 * rows, CW)
        return tn_dot(left, right)

    def l_part(k, carry):
        lo[k] = wgrad(1 - l, k).astype(BF16)
        l_copy(k).start()
        return carry

    def l_own(k, carry):
        wg[:, span(k * CW, CW)] = wgrad(l, k)
        return carry

    def l_sum(k, carry):
        l_copy(k).wait_recv()
        wg[:, span(k * CW, CW)] = wg[:, span(k * CW, CW)] + lr[k].astype(F32)
        return carry

    parts = ((0, 128), (128, 256), (384, 256))

    def m_copy(k):
        here = pl.ds(*parts[k])
        return rdma(lo2.at[:, here], lr2.at[:, here], m_send.at[k], m_recv.at[k], level)

    def part(ref, start, b, k):
        at, wide = parts[k]
        left = ref[:, :, :, span(b * block, block)].reshape(NY * 4 * rows, block)
        return tn_dot(left, gy[:, :, pl.ds(start + at, wide)].reshape(NY * 4 * rows, wide))

    def both(b, k):
        return part(sv, 0, b, k) + part(sv2, block, b, k)

    def m_all():
        for k, (at, wide) in enumerate(parts):
            wg[:, span((1 - l) * block + at, wide)] = part(sv, 0, 1 - l, k)
        for on in across2:
            on.wait_recv()
        for i in range(pieces):
            y2_copy(i, 0).wait_recv()
            r_copy(i, 1).wait_recv()
        for k, (at, wide) in enumerate(parts):
            near_sum = wg[:, span((1 - l) * block + at, wide)]
            lo2[:, pl.ds(at, wide)] = (near_sum + part(sv2, block, 1 - l, k)).astype(BF16)
            m_copy(k).start()
        for k, (at, wide) in enumerate(parts):
            wg[:, span(l * block + at, wide)] = both(l, k)
        for k, (at, wide) in enumerate(parts):
            m_copy(k).wait_recv()
            wg[:, span((1 - l) * block + at, wide)] = lr2[:, pl.ds(at, wide)].astype(F32)

    @pl.when(last)
    def _():
        m_all()

    @pl.when(jnp.logical_not(last))
    def _():
        lax.fori_loop(0, nk, l_part, 0)
        lax.fori_loop(0, nk, l_own, 0)
        lax.fori_loop(0, nk, l_sum, 0)

    mine.wait()
    for copy in home:
        copy.wait_recv()
        copy.wait_send()
    for copy in across:
        copy.wait_send()
    for a in range(2):
        w_away[a].wait_send()
    for i in range(pieces):
        for side in range(2):
            r_copy(i, side).wait_send()

    @pl.when(last)
    def _():
        for i in range(pieces):
            g2_copy(i).wait_send()
            for side in range(2):
                y0_copy(i, side).wait_send()
                y2_copy(i, side).wait_send()
        for copy in lent + across2:
            copy.wait_send()
        for k in range(len(parts)):
            m_copy(k).wait_send()

    @pl.when(jnp.logical_not(last))
    def _():
        for i in range(pieces):
            for side in range(2):
                y_copy(i, side).wait_send()
        for k in range(nk):
            l_copy(k).wait_send()
    for chip in range(2):
        for dy in range(NY):
            for b in range(2):
                if chip or dy:
                    s_copy(chip, dy, b).wait_send()

    def drain(j, carry):
        p_copy(j).wait_send()

        @pl.when(s > 0)
        def _():
            x_copy(j).wait_send()

        @pl.when(jnp.logical_not(first))
        def _():
            f_copy(j).wait_send()

        return carry

    lax.fori_loop(0, total, drain, 0)


def put_out(own_input, weight_grad, inputs_out, weights_out, sems):
    copies = [
        pltpu.make_async_copy(own_input, inputs_out.at[0], sems.at[0]),
    ]
    share = weight_grad.shape[0] // 4
    for i in range(4):
        part = pl.ds(i * share, share)
        copies.append(pltpu.make_async_copy(weight_grad.at[part], weights_out.at[0, part], sems.at[1 + i]))
    for copy in copies:
        copy.start()
    for copy in copies:
        copy.wait()


def on_device(saved, weight, out_grad):
    rows, width = out_grad.shape
    quarter, half = width // 4, width // 2
    nk = quarter // CW
    total = 4 * nk
    dma = pltpu.SemaphoreType.DMA
    vmem = pltpu.VMEM
    inside = pl.BlockSpec(memory_space=pltpu.VMEM)
    outside = pl.BlockSpec(memory_space=pltpu.HBM)
    anywhere = pl.BlockSpec(memory_space=pl.ANY)
    own_input, weight_grad = pl.pallas_call(
        relay,
        out_shape=(
            vmem((rows, width), BF16),
            vmem((quarter // 2, quarter), F32),
        ),
        in_specs=[outside, outside, outside],
        out_specs=(inside, inside),
        scratch_shapes=[
            vmem((2, quarter, half), BF16),
            vmem((4 * rows, half), BF16),
            vmem((total, rows, CW), BF16),
            vmem((total, rows, CW), BF16),
            vmem((total, rows, CW), F32),
            vmem((4 * rows, quarter), BF16),
            vmem((NY, 4 * rows, quarter), BF16),
            vmem((NY, 4, rows, quarter), BF16),
            vmem((nk, quarter // 2, CW), BF16),
            vmem((nk, quarter // 2, CW), BF16),
            vmem((NY, 4, rows, quarter), BF16),
            vmem((quarter // 2, quarter // 2), BF16),
            vmem((quarter // 2, quarter // 2), BF16),
            dma((2,)), dma((2,)), dma((2,)), dma((4,)), dma((4,)), dma((3,)), dma((3,)),
            dma((total,)), dma((total,)), dma((total,)), dma((total,)), dma((total,)), dma((total,)),
            dma((3,)), dma((3,)), dma((2, 4)), dma((2, 4)), dma((2, 4)), dma((2, 4)),
            dma((2, NY, 2)), dma((2, NY, 2)), dma((2,)), dma((2,)), dma((nk,)), dma((nk,)), dma((1,)), dma((4,)),
            dma((2, 4)), dma((2, 4)), dma((4,)), dma((4,)), dma((5,)), dma((5,)), dma((2,)), dma((2,)),
            dma((3,)), dma((3,)),
        ],
        compiler_params=pltpu.CompilerParams(
            collective_id=0, has_side_effects=True, vmem_limit_bytes=50 * 1024 * 1024
        ),
    )(out_grad, weight[0], saved[0])
    return pl.pallas_call(
        put_out,
        out_shape=(
            jax.ShapeDtypeStruct((1, rows, width), BF16),
            jax.ShapeDtypeStruct((1, quarter // 2, quarter), F32),
        ),
        in_specs=[inside, inside],
        out_specs=(outside, outside),
        scratch_shapes=[dma((5,))],
        compiler_params=pltpu.CompilerParams(vmem_limit_bytes=6 * 1024 * 1024),
    )(own_input, weight_grad)


def solution(mesh):
    placed = (
        P("section", ("dp", "tensor"), None),
        P("section", None, "tensor"),
        P(("dp", "tensor"), None),
    )
    return jax.shard_map(
        on_device,
        mesh=mesh,
        in_specs=placed,
        out_specs=(P("section", ("dp", "tensor"), None), P("section", "dp", "tensor")),
        check_vma=False,
    )
```
